128 devices in a mesh: gx: 4 (over z), gz: 16 (over x, y), gy: 2 (over core).
Axes of the slice: x: 4, y: 4, z: 4, core: 2. Of those that a mesh axis runs over, the one named last changes fastest.
Arguments:
- velocity: float32 [3, 128, 192, 2048], P(None, ('gx', 'gy'), None, 'gz'), may hold values from -6 to 6
- metric_x: float32 [128], P(('gx', 'gy')), may hold values from 0.5 to 2
- metric_y: float32 [192], replicated, may hold values from 0.5 to 2
- metric_z: float32 [2048], P('gz'), may hold values from 0.5 to 2
- x_inverse: float32 [128, 16], P(('gx', 'gy')), may hold values from -5 to 5, as said below
- y_inverse: float32 [192, 192], replicated, may hold values from -5 to 5, as said below
- z_inverse: float32 [2048, 128], P('gz'), may hold values from -5 to 5, as said below
Outputs:
- gradient: float32 [3, 3, 128, 192, 2048], P(None, None, ('gx', 'gy'), None, 'gz')
- convection: float32 [3, 128, 192, 2048], P(None, ('gx', 'gy'), None, 'gz')
The draws below stay inside these ranges and needn't reach their ends.
Inputs may be any that keep to these rules, and one draw needn't show every extreme that they name: Rows b * 16 to b * 16 + 15 of x_inverse hold the inverse of a 16 x 16 tridiagonal matrix with unit diagonal whose row r has one value between 0.2 and 0.4 on both sides of the diagonal (where they exist), drawn afresh for each row and block. y_inverse holds the inverse of such a 192 x 192 matrix. Likewise for z_inverse with blocks of 128 rows.
All inputs are finite; a program needn't handle non-finite values.
Results may differ from the reference program's by a relative error of at most 0.0003.
Values sent between devices are 32-bit elements; how exact they have to be, the bound alone decides.
A program may use at most 192 MiB of HBM per device.

```python
import math
import jax
import jax.numpy as jnp
from jax import lax

CX = 16
NY = 192
CZ = 128
NX = 128
NZ = 2048


def block_inverse(key, blocks, length):
    alphas = jax.random.uniform(key, (blocks, length), jnp.float32, 0.2, 0.4)
    indices = jnp.arange(length)
    beside = (jnp.abs(indices[:, None] - indices[None, :]) == 1).astype(jnp.float32)
    matrix = jnp.eye(length, dtype=jnp.float32)[None] + alphas[:, :, None] * beside[None]
    return jnp.linalg.inv(matrix).reshape(blocks * length, length)


def draw_x_inverse(key, part):
    return block_inverse(jax.random.fold_in(key, 11), NX // CX, CX)


def draw_y_inverse(key, part):
    return block_inverse(jax.random.fold_in(key, 23), 1, NY)


def draw_z_inverse(key, part):
    return block_inverse(jax.random.fold_in(key, 37), NZ // CZ, CZ)


def block_levels(key, dims, pieces, low, high):
    factor_of, own = 1.0, jax.random.fold_in(key, 6)
    for dim, shards_of in pieces:
        steps = jnp.exp(jax.random.uniform(jax.random.fold_in(own, dim), (shards_of,), jnp.float32, low / len(pieces), high / len(pieces)))
        factor_of = factor_of * jnp.repeat(steps, dims[dim] // shards_of).reshape([-1 if axis == dim else 1 for axis in range(len(dims))])
    return factor_of


def scatter_about(rng, shape, width, limit, cuts=(), held_as=jnp.bfloat16):
    gain = block_levels(rng, shape, cuts, -0.22, 0.18) if cuts else 1.0
    values = jax.random.normal(rng, shape, jnp.float32) * width * gain
    return jnp.minimum(jnp.maximum(values, -limit), limit).astype(held_as)


def setup_inputs(seed: int = 0) -> dict:
    key_of = jax.random.split(jax.random.key(seed), 8)
    return {
        "velocity": scatter_about(key_of[0], (3, NX, NY, NZ), 1.0, 6.0, ((1, 8), (3, 16)), jnp.float32),
        "metric_x": jnp.clip(jnp.exp(math.log(2.0) - 1.3862944 * jax.random.uniform(key_of[1], (NX,), jnp.float32) ** block_levels(key_of[1], (NX,), ((0, 8),), -0.2, 0.2)), 0.5, 2.0),
        "metric_y": jnp.clip(jnp.exp(jax.random.uniform(key_of[2], (NY,), jnp.float32, math.log(0.5), math.log(2.0))), 0.5, 2.0),
        "metric_z": jnp.clip(jnp.exp(math.log(2.0) - 1.3862944 * jax.random.uniform(key_of[3], (NZ,), jnp.float32) ** block_levels(key_of[3], (NZ,), ((0, 16),), -0.2, 0.2)), 0.5, 2.0),
        "x_inverse": draw_x_inverse(jax.random.fold_in(key_of[7], 71), 0),
        "y_inverse": draw_y_inverse(jax.random.fold_in(key_of[7], 71), 0),
        "z_inverse": draw_z_inverse(jax.random.fold_in(key_of[7], 71), 0),
    }


COUPLING = 1.0 / 3.0
NEAR_WEIGHT = 7.0 / 9.0
FAR_WEIGHT = 1.0 / 36.0

def stencil(values, axis_of, periodic):
    length = values.shape[axis_of]
    if periodic:

        def shifted(offset):
            return jnp.roll(values, -offset, axis=axis_of)
    else:
        widths = [(0, 0)] * values.ndim
        widths[axis_of] = (2, 2)
        padded = jnp.pad(values, widths)

        def shifted(offset):
            return lax.slice_in_dim(padded, 2 + offset, 2 + offset + length, axis=axis_of)
    return NEAR_WEIGHT * (shifted(1) - shifted(-1)) + FAR_WEIGHT * (shifted(2) - shifted(-2))

def line_solve(source, inverse, axis_of, periodic):
    length = source.shape[axis_of]
    block_size = inverse.shape[1]
    blocks = length // block_size
    moved_source = jnp.moveaxis(source, axis_of, 0)
    rest_shape = moved_source.shape[1:]
    line_view = moved_source.reshape(blocks, block_size, -1)
    inverses = inverse.reshape(blocks, block_size, block_size)
    inside = jnp.einsum('pij,pjl->pil', inverses, line_view, precision=lax.Precision.HIGHEST)
    system = jnp.eye(2 * blocks, dtype=jnp.float32)
    for block_index in range(blocks):
        left_block = block_index - 1
        right_block = block_index + 1
        if periodic:
            left_block = left_block % blocks
            right_block = right_block % blocks
        if left_block >= 0:
            system = system.at[2 * block_index, 2 * left_block + 1].add(COUPLING * inverses[block_index, 0, 0])
            system = system.at[2 * block_index + 1, 2 * left_block + 1].add(COUPLING * inverses[block_index, block_size - 1, 0])
        if right_block < blocks:
            system = system.at[2 * block_index, 2 * right_block].add(COUPLING * inverses[block_index, 0, block_size - 1])
            system = system.at[2 * block_index + 1, 2 * right_block].add(COUPLING * inverses[block_index, block_size - 1, block_size - 1])
    end_values = jnp.stack([inside[:, 0], inside[:, block_size - 1]], axis=1).reshape(2 * blocks, -1)
    solved = jnp.linalg.solve(system, end_values).reshape(blocks, 2, -1)
    starts = solved[:, 0]
    finals = solved[:, 1]
    if periodic:
        left_final = jnp.roll(finals, 1, axis=0)
        right_start = jnp.roll(starts, -1, axis=0)
    else:
        zero_row = jnp.zeros_like(finals[:1])
        left_final = jnp.concatenate([zero_row, finals[:-1]], axis=0)
        right_start = jnp.concatenate([starts[1:], zero_row], axis=0)
    result = inside - COUPLING * inverses[:, :, 0:1] * left_final[:, None, :] - COUPLING * inverses[:, :, block_size - 1:] * right_start[:, None, :]
    return jnp.moveaxis(result.reshape((length,) + rest_shape), 0, axis_of)

def derivative(values, inverse, metric, axis_of, periodic):
    slope = line_solve(stencil(values, axis_of, periodic), inverse, axis_of, periodic)
    layout = [1] * values.ndim
    layout[axis_of] = metric.shape[0]
    return slope * metric.reshape(layout)

def reference(velocity, metric_x, metric_y, metric_z, x_inverse, y_inverse, z_inverse):
    settings = ((metric_x, x_inverse, True), (metric_y, y_inverse, False), (metric_z, z_inverse, True))
    convection = [jnp.zeros_like(velocity[0]) for component in range(3)]
    gradient_rows = []
    for direction in range(3):
        metric, inverse, periodic = settings[direction]
        per_component = []
        for component in range(3):
            per_component.append(derivative(velocity[component], inverse, metric, direction, periodic))
            product = velocity[component] * velocity[direction]
            convection[component] = convection[component] + derivative(product, inverse, metric, direction, periodic)
        gradient_rows.append(jnp.stack(per_component))
    gradient = jnp.stack(gradient_rows, axis=1)
    return (gradient, jnp.stack(convection))
```

```python
import functools

import jax
import jax.numpy as jnp
from jax import lax
from jax.experimental import pallas as pl
from jax.experimental.pallas import tpu as pltpu
from jax.sharding import PartitionSpec as P

COUPLING = 1.0 / 3.0
NEAR = 7.0 / 9.0
FAR = 1.0 / 36.0
F32 = jnp.float32
BF16 = jnp.bfloat16
MESH = pl.DeviceIdType.MESH
HIGH = lax.Precision.HIGHEST
CHUNKS = 2
MIB = 1 << 20


def split(values):
    high = values.astype(BF16)
    return high, (values - high.astype(F32)).astype(BF16)


def iota(shape, dim):
    return lax.broadcasted_iota(jnp.int32, shape, dim)


def band(size):
    step = iota((size, size), 1) - iota((size, size), 0)
    near = jnp.where(step == 1, NEAR, jnp.where(step == -1, -NEAR, 0.0))
    far = jnp.where(step == 2, FAR, jnp.where(step == -2, -FAR, 0.0))
    return (near + far).astype(F32)


def dot(a, b, dims=((1,), (0,)), precision=None):
    return lax.dot_general(a, b, (dims, ((), ())), precision=precision, preferred_element_type=F32)


def tap(row, j, size):
    def at(k):
        return row(k) if 0 <= k < size else None

    total = None
    for k, weight in ((j - 1, NEAR), (j + 1, -NEAR), (j - 2, FAR), (j + 2, -FAR)):
        value = at(k)
        if value is not None:
            total = weight * value if total is None else total + weight * value
    return total


def z_select(z_inverse, store):
    size = z_inverse.shape[0]
    local = dot(z_inverse, band(size), precision=HIGH)
    first, last = local[0:1], local[size - 1 : size]
    row, col = iota((32, size), 0), iota((32, size), 1)
    for field in range(6):
        rows = jnp.where(row == 16 + field, first, 0.0) + jnp.where(row == 24 + field, last, 0.0)
        if field < 3:
            for place, cell in ((field, 0), (3 + field, 1), (8 + field, size - 2), (11 + field, size - 1)):
                rows = jnp.where((row == place) & (col == cell), 1.0, rows)
        high, low = split(rows)
        both = jnp.concatenate([high, low], axis=0)
        store[field] = jnp.concatenate([both, both], axis=1)


def z_end_weights(z_inverse):
    size = z_inverse.shape[0]
    row, col = iota((16, 32), 0), iota((16, 32), 1)
    weights = jnp.zeros((16, 32), F32)
    for end, line in ((0, 0), (8, size - 1)):
        ends = [z_inverse[line : line + 1, k : k + 1] for k in (0, 1, size - 2, size - 1)]
        terms = (
            (0, -FAR * ends[0]),
            (3, -NEAR * ends[0] - FAR * ends[1]),
            (16, NEAR * ends[3] + FAR * ends[2]),
            (19, FAR * ends[3]),
        )
        for field in range(6):
            base = field % 3 + (0 if field < 3 else 8)
            for place, value in terms:
                weights = jnp.where((row == end + field) & (col == base + place), value, weights)
    return weights


def exchange_kernel(
    v_hbm, x_inv, z_inv,
    z_rows, xh, xp, xe, xc,
    vv, sel, zs1, zs2, zh, zp, xcs, wtab,
    load_sem, x1s, x1r, x2s, x2r, z1s, z1r, z2s, z2r, xcsem, xcrecv,
):
    gx, gy, gz = lax.axis_index("gx"), lax.axis_index("gy"), lax.axis_index("gz")
    nx, ny, nz = lax.axis_size("gx"), lax.axis_size("gy"), lax.axis_size("gz")
    me = gx * ny + gy
    count = nx * ny
    xl, xr = lax.rem(me + count - 1, count), lax.rem(me + 1, count)
    left = {"gx": xl // ny, "gy": lax.rem(xl, ny)}
    right = {"gx": xr // ny, "gy": lax.rem(xr, ny)}
    below = {"gz": lax.rem(gz + nz - 1, nz)}
    above = {"gz": lax.rem(gz + 1, nz)}
    barrier = pltpu.get_barrier_semaphore()
    for device in (left, right, below, above):
        pl.semaphore_signal(barrier, inc=1, device_id=device, device_id_type=MESH)

    cx, rows, cz = vv.shape[1:]
    loads = [pltpu.make_async_copy(v_hbm.at[i], vv.at[i], load_sem.at[i]) for i in range(3)]
    for load in loads:
        load.start()
    tile = (8, 128)
    xcs[0] = jnp.full(tile, x_inv[0, 0], F32)
    xcs[1] = jnp.full(tile, x_inv[cx - 1, cx - 1], F32)
    for end, line in ((0, 0), (1, cx - 1)):
        for j in range(-2, cx + 2):
            wtab[end * (cx + 4) + j + 2] = jnp.full(tile, tap(lambda k: x_inv[line, k], j, cx), F32)
    pl.semaphore_wait(barrier, 4)

    def send(src, dst, s, r, device):
        return pltpu.make_async_remote_copy(
            src_ref=src, dst_ref=dst, send_sem=s, recv_sem=r, device_id=device, device_id_type=MESH)

    step = rows // CHUNKS
    faces = []
    for c in range(CHUNKS):
        part = pl.ds(c * step, step)
        pair = (
            send(v_hbm.at[:, pl.ds(cx - 2, 2), part], xh.at[0, :, :, part], x1s.at[0, c], x1r.at[0, c], right),
            send(v_hbm.at[:, pl.ds(0, 2), part], xh.at[1, :, :, part], x1s.at[1, c], x1r.at[1, c], left),
        )
        for copy in pair:
            copy.start()
        faces.append(pair)
    corners = (
        send(xcs.at[1], xc.at[0], xcsem.at[0], xcrecv.at[0], right),
        send(xcs.at[0], xc.at[1], xcsem.at[1], xcrecv.at[1], left),
    )
    for copy in corners:
        copy.start()

    zi = z_inv[...]
    z_select(zi, sel)
    size = zi.shape[0]
    corner = (zi[0:1, 0:1], zi[size - 1 : size, size - 1 : size])
    for load in loads:
        load.wait()

    @pl.loop(0, cx)
    def _(x):
        v = [vv[i, x] for i in range(3)]
        total = jnp.zeros((64, rows), F32)
        for field in range(6):
            value = v[field] if field < 3 else v[field - 3] * v[2]
            total = total + dot(sel[field], jnp.concatenate(split(value), axis=1), ((1,), (1,)))
        got = total[0:32] + total[32:64]
        spare = iota((8, rows), 0) == 6
        zs1[0, x] = jnp.where(spare, corner[0], got[0:8])
        zs1[1, x] = jnp.where(spare, corner[1], got[8:16])
        zs2[0, x] = got[16:24]
        zs2[1, x] = got[24:32]

    z_faces = (
        send(zs1.at[1], zh.at[0], z1s.at[0], z1r.at[0], above),
        send(zs1.at[0], zh.at[1], z1s.at[1], z1r.at[1], below),
    )
    for copy in z_faces:
        copy.start()

    @pl.loop(0, rows // 8)
    def _(t):
        part = pl.ds(pl.multiple_of(t * 8, 8), 8)
        ends = [[None] * 6, [None] * 6]
        for j in range(cx):
            v = [vv[i, j, part] for i in range(3)]
            fields = v + [a * v[0] for a in v]
            for end in range(2):
                weight = wtab[end * (cx + 4) + j + 2]
                for f in range(6):
                    term = weight * fields[f]
                    ends[end][f] = term if ends[end][f] is None else ends[end][f] + term
        for end in range(2):
            for f in range(6):
                xe[end, f, part] = ends[end][f]

    for copy in z_faces:
        copy.wait()
    wz = split(z_end_weights(zi))
    wz = jnp.concatenate([wz[0], wz[0], wz[1]], axis=1)

    @pl.loop(0, cx)
    def _(x):
        row = iota((8, rows), 0)
        halo = []
        for side in range(2):
            h = zh[side, x]
            halo += [h, h * jnp.where(row < 3, h[2:3], h[5:6])]
        halo = jnp.concatenate(halo, axis=0)
        high, low = split(halo)
        more = dot(wz, jnp.concatenate([high, low, high], axis=0))
        z_rows[x, 0:32] = halo
        first = zs2[0, x] + more[0:8]
        last = zs2[1, x] + more[8:16]
        zs2[0, x] = first
        zs2[1, x] = last
        z_rows[x, 48:56] = first
        z_rows[x, 56:64] = last

    z_ends = (
        send(zs2.at[1], zp.at[0], z2s.at[0], z2r.at[0], above),
        send(zs2.at[0], zp.at[1], z2s.at[1], z2r.at[1], below),
    )
    for copy in z_ends:
        copy.start()

    x_ends = []
    for c in range(CHUNKS):
        for copy in faces[c]:
            copy.wait()

        @pl.loop(0, step // 8)
        def _(t):
            part = pl.ds(pl.multiple_of(c * step + t * 8, 8), 8)
            ends = [[xe[end, f, part] for f in range(6)] for end in range(2)]
            for side in range(2):
                for layer in range(2):
                    j = layer - 2 if side == 0 else cx + layer
                    v = [xh[side, i, layer, part] for i in range(3)]
                    fields = v + [a * v[0] for a in v]
                    for end in range(2):
                        weight = wtab[end * (cx + 4) + j + 2]
                        for f in range(6):
                            ends[end][f] = ends[end][f] + weight * fields[f]
            for end in range(2):
                for f in range(6):
                    xe[end, f, part] = ends[end][f]

        part = pl.ds(c * step, step)
        pair = (
            send(xe.at[1, :, part], xp.at[0, :, part], x2s.at[0, c], x2r.at[0, c], right),
            send(xe.at[0, :, part], xp.at[1, :, part], x2s.at[1, c], x2r.at[1, c], left),
        )
        for copy in pair:
            copy.start()
        x_ends.append(pair)

    for copy in z_ends:
        copy.wait()
    for side in range(2):
        z_rows[:, 32 + 8 * side : 40 + 8 * side] = zp[side]
    for copy in corners:
        copy.wait()
    for pair in x_ends:
        for copy in pair:
            copy.wait()


def exchange(velocity, x_inverse, z_inverse):
    _, cx, rows, cz = velocity.shape
    vmem = pl.BlockSpec(memory_space=pltpu.VMEM)
    dma = pltpu.SemaphoreType.DMA
    return pl.pallas_call(
        exchange_kernel,
        out_shape=(
            jax.ShapeDtypeStruct((cx, 64, rows), F32),
            jax.ShapeDtypeStruct((2, 3, 2, rows, cz), F32),
            jax.ShapeDtypeStruct((2, 6, rows, cz), F32),
            jax.ShapeDtypeStruct((2, 6, rows, cz), F32),
            jax.ShapeDtypeStruct((2, 8, 128), F32),
        ),
        in_specs=[
            pl.BlockSpec(memory_space=pl.ANY),
            pl.BlockSpec(memory_space=pltpu.SMEM),
            vmem,
        ],
        out_specs=(vmem,) * 5,
        scratch_shapes=[
            pltpu.VMEM((3, cx, rows, cz), F32),
            pltpu.VMEM((6, 64, 2 * cz), BF16),
            pltpu.VMEM((2, cx, 8, rows), F32),
            pltpu.VMEM((2, cx, 8, rows), F32),
            pltpu.VMEM((2, cx, 8, rows), F32),
            pltpu.VMEM((2, cx, 8, rows), F32),
            pltpu.VMEM((2, 8, 128), F32),
            pltpu.VMEM((2 * (cx + 4), 8, 128), F32),
            dma((3,)),
            dma((2, CHUNKS)), dma((2, CHUNKS)), dma((2, CHUNKS)), dma((2, CHUNKS)),
            dma((2,)), dma((2,)), dma((2,)), dma((2,)), dma((2,)), dma((2,)),
        ],
        compiler_params=pltpu.CompilerParams(
            collective_id=0, has_side_effects=True, vmem_limit_bytes=20 * MIB),
        name="exchange",
    )(velocity, x_inverse, z_inverse)


def z_tables(z_inverse, metric, tail_left, first_right, weights, spread):
    size = z_inverse.shape[0]
    local = dot(z_inverse, band(size), precision=HIGH)
    high, low = split(local.T * metric)
    both = jnp.concatenate([high, low], axis=1)
    weights[...] = jnp.concatenate([both, both], axis=0)
    columns = z_inverse.T
    c0, c1 = columns[0:1] * metric, columns[1:2] * metric
    c2, c3 = columns[size - 2 : size - 1] * metric, columns[size - 1 : size] * metric
    own_first, own_last = columns[0:1, 0:1], columns[size - 1 : size, size - 1 : size]
    scale_left = COUPLING / (1.0 - COUPLING * COUPLING * tail_left * own_first)
    scale_right = COUPLING / (1.0 - COUPLING * COUPLING * own_last * first_right)
    row = iota((64, size), 0)
    for field in range(6):
        base = field % 3 + (0 if field < 3 else 8)
        terms = (
            (base, -FAR * c0),
            (base + 3, -NEAR * c0 - FAR * c1),
            (base + 16, NEAR * c3 + FAR * c2),
            (base + 19, FAR * c3),
            (32 + field, -scale_left * c0),
            (40 + field, -scale_right * c3),
            (48 + field, COUPLING * tail_left * scale_left * c0),
            (56 + field, COUPLING * first_right * scale_right * c3),
        )
        table = jnp.zeros((64, size), F32)
        for place, value in terms:
            table = jnp.where(row == place, value, table)
        high, low = split(table)
        spread[:, field * size : (field + 1) * size] = jnp.concatenate([high, high, low], axis=0)


def y_table(y_inverse, metric):
    size = y_inverse.shape[0]
    own = iota((size, size), 0) == iota((size, size), 1)
    column = jnp.sum(jnp.where(own, metric, 0.0), axis=1, keepdims=True)
    high, low = split(dot(y_inverse, band(size), precision=HIGH) * column)
    return jnp.concatenate([high, high, low], axis=1)


def yz_kernel(v_ref, rows_ref, yi, my, zi, mz, corner, grad, conv, ytab, ztab, spread):
    @pl.when(pl.program_id(0) == 0)
    def _():
        ytab[...] = y_table(yi[...], my[...])
        z_tables(zi[...], mz[...], corner[0, 6:7, 0:1], corner[1, 6:7, 0:1], ztab, spread)

    pair, rows, cz = v_ref.shape[1:]
    v = [[v_ref[i, x] for x in range(pair)] for i in range(3)]
    parts = [[split(v[i][x]) for x in range(pair)] for i in range(3)]

    def along_y(piece):
        high = jnp.concatenate([p[0] for p in piece], axis=1)
        low = jnp.concatenate([p[1] for p in piece], axis=1)
        return dot(ytab[...], jnp.concatenate([high, low, high], axis=0))

    def along_z(piece, x, field):
        got = dot(jnp.concatenate(piece, axis=1), ztab[...])
        return got[:, :cz] + got[:, cz:]

    extra = []
    for x in range(pair):
        high, low = split(rows_ref[x])
        extra.append(dot(jnp.concatenate([high, low, high], axis=0), spread[...], ((0,), (0,))))
    for i in range(3):
        got = along_y(parts[i])
        for x in range(pair):
            grad[0, i, x] = got[:, x * cz : (x + 1) * cz]
        got = along_y([split(v[i][x] * v[1][x]) for x in range(pair)])
        for x in range(pair):
            grad[1, i, x] = along_z(parts[i][x], x, i) + extra[x][:, i * cz : (i + 1) * cz]
            second = along_z(split(v[i][x] * v[2][x]), x, 3 + i)
            conv[i, x] = got[:, x * cz : (x + 1) * cz] + (second + extra[x][:, (3 + i) * cz : (4 + i) * cz])


def yz(velocity, z_rows, y_inverse, metric_y, z_inverse, metric_z):
    _, cx, rows, cz = velocity.shape
    pair = 2
    return pl.pallas_call(
        yz_kernel,
        grid=(cx // pair,),
        out_shape=(
            jax.ShapeDtypeStruct((2, 3, cx, rows, cz), F32),
            jax.ShapeDtypeStruct((3, cx, rows, cz), F32),
        ),
        in_specs=[
            pl.BlockSpec((3, pair, rows, cz), lambda x: (0, x, 0, 0)),
            pl.BlockSpec((pair, 64, rows), lambda x: (x, 0, 0)),
            pl.BlockSpec((rows, rows), lambda x: (0, 0)),
            pl.BlockSpec((1, rows), lambda x: (0, 0)),
            pl.BlockSpec((cz, cz), lambda x: (0, 0)),
            pl.BlockSpec((1, cz), lambda x: (0, 0)),
            pl.BlockSpec((2, 8, 128), lambda x: (0, 0, 0)),
        ],
        out_specs=(
            pl.BlockSpec((2, 3, pair, rows, cz), lambda x: (0, 0, x, 0, 0)),
            pl.BlockSpec((3, pair, rows, cz), lambda x: (0, x, 0, 0)),
        ),
        scratch_shapes=[
            pltpu.VMEM((rows, 3 * rows), BF16),
            pltpu.VMEM((2 * cz, 2 * cz), BF16),
            pltpu.VMEM((192, 6 * cz), BF16),
        ],
        compiler_params=pltpu.CompilerParams(vmem_limit_bytes=20 * MIB),
        name="yz",
    )(velocity, z_rows, y_inverse, metric_y.reshape(1, rows), z_inverse, metric_z.reshape(1, cz),
      jnp.stack([z_rows[0, 0:8, 0:128], z_rows[0, 16:24, 0:128]]))


def x_kernel(v_ref, xh, xp, xe, xc, x_inv, mx, gyz, cyz, grad, conv, tab):
    cx = v_ref.shape[1]
    tile = (8, 128)

    @pl.when(pl.program_id(0) == 0)
    def _():
        def full(value):
            return jnp.full(tile, value, F32)

        def inv(i, j):
            return full(x_inv[i, j])

        before = None
        for i in range(cx):
            metric = full(mx[i])
            if i < cx - 1:
                up = inv(i, i + 1) / inv(i + 1, i + 1)
                own = inv(i, i) - up * inv(i + 1, i)
                tab[2 * cx + i] = up * metric / full(mx[i + 1])
            else:
                own = inv(i, i)
            if i > 0:
                down = inv(i, i - 1)
                if i < cx - 1:
                    down = down - up * inv(i + 1, i - 1)
                tab[cx + i] = down / before * metric / full(mx[i - 1])
            tab[i] = NEAR * metric * own
            before = own
        square = COUPLING * COUPLING
        for side, corner in ((0, inv(0, 0)), (1, inv(cx - 1, cx - 1))):
            other = xc[side]
            scale = (COUPLING / NEAR) / (1.0 - square * other * corner)
            tab[3 * cx + 2 * side] = scale
            tab[3 * cx + 2 * side + 1] = COUPLING * other * scale

    @pl.loop(0, v_ref.shape[2] // 8)
    def _(t):
        part = pl.ds(pl.multiple_of(t * 8, 8), 8)

        def cell(j):
            if j < 0:
                v = [xh[0, i, j + 2, part] for i in range(3)]
            elif j >= cx:
                v = [xh[1, i, j - cx, part] for i in range(3)]
            else:
                v = [v_ref[i, j, part] for i in range(3)]
            return v + [a * v[0] for a in v]

        window = [cell(j) for j in range(-2, 2)]
        state = None
        for j in range(cx):
            window.append(cell(j + 2))
            fresh = []
            for f in range(6):
                d = (window[3][f] - window[1][f]) + (FAR / NEAR) * (window[4][f] - window[0][f])
                for side, line in ((0, 0), (1, cx - 1)):
                    if j == line:
                        k = 3 * cx + 2 * side
                        d = d - tab[k] * xp[side, f, part] + tab[k + 1] * xe[side, f, part]
                value = tab[j] * d
                if state is not None:
                    value = value + tab[cx + j] * state[f]
                fresh.append(value)
                if j < cx - 1:
                    if f < 3:
                        grad[f, 0, j, part] = value
                    else:
                        conv[f - 3, j, part] = value
            state = fresh
            window.pop(0)
        for j in range(cx - 1, -1, -1):
            if j < cx - 1:
                up = tab[2 * cx + j]
                state = [
                    (grad[f, 0, j, part] if f < 3 else conv[f - 3, j, part]) + up * state[f]
                    for f in range(6)
                ]
            for i in range(3):
                grad[i, 0, j, part] = state[i]
                grad[i, 1, j, part] = gyz[0, i, j, part]
                grad[i, 2, j, part] = gyz[1, i, j, part]
                conv[i, j, part] = state[3 + i] + cyz[i, j, part]


def x_solve(velocity, xh, xp, xe, xc, x_inverse, metric_x, gyz, cyz):
    _, cx, rows, cz = velocity.shape
    step = 16
    smem = pl.BlockSpec(memory_space=pltpu.SMEM)
    return pl.pallas_call(
        x_kernel,
        grid=(rows // step,),
        out_shape=(
            jax.ShapeDtypeStruct((3, 3, cx, rows, cz), F32),
            jax.ShapeDtypeStruct((3, cx, rows, cz), F32),
        ),
        in_specs=[
            pl.BlockSpec((3, cx, step, cz), lambda y: (0, 0, y, 0)),
            pl.BlockSpec((2, 3, 2, step, cz), lambda y: (0, 0, 0, y, 0)),
            pl.BlockSpec((2, 6, step, cz), lambda y: (0, 0, y, 0)),
            pl.BlockSpec((2, 6, step, cz), lambda y: (0, 0, y, 0)),
            pl.BlockSpec((2, 8, 128), lambda y: (0, 0, 0)),
            smem,
            smem,
            pl.BlockSpec((2, 3, cx, step, cz), lambda y: (0, 0, 0, y, 0)),
            pl.BlockSpec((3, cx, step, cz), lambda y: (0, 0, y, 0)),
        ],
        out_specs=(
            pl.BlockSpec((3, 3, cx, step, cz), lambda y: (0, 0, 0, y, 0)),
            pl.BlockSpec((3, cx, step, cz), lambda y: (0, 0, y, 0)),
        ),
        scratch_shapes=[pltpu.VMEM((3 * cx + 4, 8, 128), F32)],
        compiler_params=pltpu.CompilerParams(vmem_limit_bytes=20 * MIB),
        name="x_solve",
    )(velocity, xh, xp, xe, xc, x_inverse, metric_x, gyz, cyz)


def on_device(velocity, metric_x, metric_y, metric_z, x_inverse, y_inverse, z_inverse):
    z_rows, xh, xp, xe, xc = exchange(velocity, x_inverse, z_inverse)
    gyz, cyz = yz(velocity, z_rows, y_inverse, metric_y, z_inverse, metric_z)
    return tuple(x_solve(velocity, xh, xp, xe, xc, x_inverse, metric_x, gyz, cyz))


def solution(mesh):
    return jax.shard_map(
        on_device,
        mesh=mesh,
        in_specs=(
            P(None, ("gx", "gy"), None, "gz"),
            P(("gx", "gy")),
            P(),
            P("gz"),
            P(("gx", "gy"), None),
            P(),
            P("gz", None),
        ),
        out_specs=(P(None, None, ("gx", "gy"), None, "gz"), P(None, ("gx", "gy"), None, "gz")),
        check_vma=False,
    )
```

```python
import jax
import jax.numpy as jnp
from jax import lax
from jax.experimental import pallas as pl
from jax.experimental.pallas import tpu as pltpu
from jax.sharding import PartitionSpec as P

COUPLING = 1.0 / 3.0
NEAR = 7.0 / 9.0
FAR = 1.0 / 36.0
F32 = jnp.float32
BF16 = jnp.bfloat16
MESH = pl.DeviceIdType.MESH
HIGH = lax.Precision.HIGHEST
CHUNKS = 2
BETWEEN = 1
OUT_CHUNKS = 6
MIB = 1 << 20


def split(values):
    high = values.astype(BF16)
    return high, (values - high.astype(F32)).astype(BF16)


def iota(shape, dim):
    return lax.broadcasted_iota(jnp.int32, shape, dim)


def band(size):
    step = iota((size, size), 1) - iota((size, size), 0)
    near = jnp.where(step == 1, NEAR, jnp.where(step == -1, -NEAR, 0.0))
    far = jnp.where(step == 2, FAR, jnp.where(step == -2, -FAR, 0.0))
    return (near + far).astype(F32)


def dot(a, b, dims=((1,), (0,)), precision=None):
    return lax.dot_general(a, b, (dims, ((), ())), precision=precision, preferred_element_type=F32)


def tap(line, j):
    size = line.shape[1]
    total = jnp.zeros((1, 1), F32)
    for k, weight in ((j - 1, NEAR), (j + 1, -NEAR), (j - 2, FAR), (j + 2, -FAR)):
        if 0 <= k < size:
            total = total + weight * line[:, k : k + 1]
    return total


def full(value):
    return jnp.broadcast_to(value, (8, 128))


def z_select(z_inverse, store):
    size = z_inverse.shape[0]
    local = dot(z_inverse, band(size), precision=HIGH)
    first, last = local[0:1], local[size - 1 : size]
    row, col = iota((32, size), 0), iota((32, size), 1)
    for field in range(6):
        rows = jnp.where(row == 16 + field, first, 0.0) + jnp.where(row == 24 + field, last, 0.0)
        if field < 3:
            for place, cell in ((field, 0), (3 + field, 1), (8 + field, size - 2), (11 + field, size - 1)):
                rows = jnp.where((row == place) & (col == cell), 1.0, rows)
        high, low = split(rows)
        both = jnp.concatenate([high, low], axis=0)
        store[field] = jnp.concatenate([both, both], axis=1)


def z_end_weights(z_inverse):
    size = z_inverse.shape[0]
    row, col = iota((16, 32), 0), iota((16, 32), 1)
    weights = jnp.zeros((16, 32), F32)
    for end, line in ((0, 0), (8, size - 1)):
        ends = [z_inverse[line : line + 1, k : k + 1] for k in (0, 1, size - 2, size - 1)]
        terms = (
            (0, -FAR * ends[0]),
            (3, -NEAR * ends[0] - FAR * ends[1]),
            (16, NEAR * ends[3] + FAR * ends[2]),
            (19, FAR * ends[3]),
        )
        for field in range(6):
            base = field % 3 + (0 if field < 3 else 8)
            for place, value in terms:
                weights = jnp.where((row == end + field) & (col == base + place), value, weights)
    return weights


def z_tables(z_inverse, metric, tail_left, first_right, weights, spread):
    size = z_inverse.shape[0]
    local = dot(z_inverse, band(size), precision=HIGH)
    high, low = split(local.T * metric)
    both = jnp.concatenate([high, low], axis=1)
    weights[...] = jnp.concatenate([both, both], axis=0)
    columns = z_inverse.T
    c0, c1 = columns[0:1] * metric, columns[1:2] * metric
    c2, c3 = columns[size - 2 : size - 1] * metric, columns[size - 1 : size] * metric
    own_first, own_last = columns[0:1, 0:1], columns[size - 1 : size, size - 1 : size]
    scale_left = COUPLING / (1.0 - COUPLING * COUPLING * tail_left * own_first)
    scale_right = COUPLING / (1.0 - COUPLING * COUPLING * own_last * first_right)
    row = iota((64, size), 0)
    for field in range(6):
        base = field % 3 + (0 if field < 3 else 8)
        terms = (
            (base, -FAR * c0),
            (base + 3, -NEAR * c0 - FAR * c1),
            (base + 16, NEAR * c3 + FAR * c2),
            (base + 19, FAR * c3),
            (32 + field, -scale_left * c0),
            (40 + field, -scale_right * c3),
            (48 + field, COUPLING * tail_left * scale_left * c0),
            (56 + field, COUPLING * first_right * scale_right * c3),
        )
        table = jnp.zeros((64, size), F32)
        for place, value in terms:
            table = jnp.where(row == place, value, table)
        high, low = split(table)
        spread[:, field * size : (field + 1) * size] = jnp.concatenate([high, high, low], axis=0)


def y_table(y_inverse, metric):
    size = y_inverse.shape[0]
    own = iota((size, size), 0) == iota((size, size), 1)
    column = jnp.sum(jnp.where(own, metric, 0.0), axis=1, keepdims=True)
    high, low = split(dot(y_inverse, band(size), precision=HIGH) * column)
    return jnp.concatenate([high, high, low], axis=1)


def x_end_weights(inverse, store):
    size = inverse.shape[0]
    for end, line in ((0, 0), (1, size - 1)):
        for j in range(-2, size + 2):
            store[end * (size + 4) + j + 2] = full(tap(inverse[line : line + 1], j))


def x_tables(inverse, metric, corners, tab):
    size = inverse.shape[0]

    def inv(i, j):
        return inverse[i : i + 1, j : j + 1]

    before = None
    for i in range(size):
        scale = metric[:, i : i + 1]
        if i < size - 1:
            up = inv(i, i + 1) / inv(i + 1, i + 1)
            own = inv(i, i) - up * inv(i + 1, i)
            tab[2 * size + i] = full(up * scale / metric[:, i + 1 : i + 2])
        else:
            own = inv(i, i)
        if i > 0:
            down = inv(i, i - 1)
            if i < size - 1:
                down = down - up * inv(i + 1, i - 1)
            tab[size + i] = full(down / before * scale / metric[:, i - 1 : i])
        tab[i] = full(NEAR * scale * own)
        before = own
    for side, corner in ((0, inv(0, 0)), (1, inv(size - 1, size - 1))):
        other = corners[side]
        scale = (COUPLING / NEAR) / (1.0 - COUPLING * COUPLING * other * full(corner))
        tab[3 * size + 2 * side] = scale
        tab[3 * size + 2 * side + 1] = COUPLING * other * scale


def z_local(x, v, sel, corner, parts, zs1, zs2):
    rows = v.shape[2]
    velocity = [v[i, x] for i in range(3)]
    total = jnp.zeros((64, rows), F32)
    for field in range(6):
        value = velocity[field] if field < 3 else velocity[field - 3] * velocity[2]
        piece = jnp.concatenate(split(value), axis=1)
        parts[field, x] = piece
        total = total + dot(sel[field], piece, ((1,), (1,)))
    got = total[0:32] + total[32:64]
    spare = iota((8, rows), 0) == 6
    zs1[0, x] = jnp.where(spare, corner[0], got[0:8])
    zs1[1, x] = jnp.where(spare, corner[1], got[8:16])
    zs2[0, x] = got[16:24]
    zs2[1, x] = got[24:32]


def z_halo(x, zh, wz, z_rows, zs2):
    rows = zh.shape[3]
    row = iota((8, rows), 0)
    halo = []
    for side in range(2):
        h = zh[side, x]
        halo += [h, h * jnp.where(row < 3, h[2:3], h[5:6])]
    halo = jnp.concatenate(halo, axis=0)
    high, low = split(halo)
    more = dot(wz, jnp.concatenate([high, low, high], axis=0))
    z_rows[x, 0:32] = halo
    first = zs2[0, x] + more[0:8]
    last = zs2[1, x] + more[8:16]
    zs2[0, x] = first
    zs2[1, x] = last
    z_rows[x, 48:56] = first
    z_rows[x, 56:64] = last


def x_local(t, v, wtab, xe):
    part = pl.ds(pl.multiple_of(t * 8, 8), 8)
    size = v.shape[1]
    ends = [[None] * 6, [None] * 6]
    for j in range(size):
        velocity = [v[i, j, part] for i in range(3)]
        fields = velocity + [a * velocity[0] for a in velocity]
        for end in range(2):
            weight = wtab[end * (size + 4) + j + 2]
            for f in range(6):
                term = weight * fields[f]
                ends[end][f] = term if ends[end][f] is None else ends[end][f] + term
    for end in range(2):
        for f in range(6):
            xe[end, f, part] = ends[end][f]


def x_halo(t, size, xh, wtab, xe):
    part = pl.ds(pl.multiple_of(t * 8, 8), 8)
    ends = [[xe[end, f, part] for f in range(6)] for end in range(2)]
    for side in range(2):
        for layer in range(2):
            j = layer - 2 if side == 0 else size + layer
            velocity = [xh[side, i, layer, part] for i in range(3)]
            fields = velocity + [a * velocity[0] for a in velocity]
            for end in range(2):
                weight = wtab[end * (size + 4) + j + 2]
                for f in range(6):
                    ends[end][f] = ends[end][f] + weight * fields[f]
    for end in range(2):
        for f in range(6):
            xe[end, f, part] = ends[end][f]


def along_y(p, v, parts, ytab, gyz, cyz):
    cz = v.shape[3]
    planes = (2 * p, 2 * p + 1)

    def apply(pieces):
        high = jnp.concatenate([a[0] for a in pieces], axis=1)
        low = jnp.concatenate([a[1] for a in pieces], axis=1)
        return dot(ytab[...], jnp.concatenate([high, low, high], axis=0))

    def held(field):
        got = [parts[field, x] for x in planes]
        return [(g[:, :cz], g[:, cz:]) for g in got]

    for i in range(3):
        got = apply(held(i))
        for k, x in enumerate(planes):
            gyz[0, i, x] = got[:, k * cz : (k + 1) * cz]
        got = apply(held(4) if i == 2 else [split(v[i, x] * v[1, x]) for x in planes])
        for k, x in enumerate(planes):
            cyz[i, x] = got[:, k * cz : (k + 1) * cz]


def along_z(x, parts, ztab, spread, z_rows, gyz, cyz):
    cz = gyz.shape[4]
    high, low = split(z_rows[x])
    extra = dot(jnp.concatenate([high, low, high], axis=0), spread[...], ((0,), (0,)))
    for field in range(6):
        got = dot(parts[field, x], ztab[...])
        got = got[:, :cz] + got[:, cz:] + extra[:, field * cz : (field + 1) * cz]
        if field < 3:
            gyz[1, field, x] = got
        else:
            cyz[field - 3, x] = cyz[field - 3, x] + got


def exchange_kernel(
    v_hbm, xi_hbm, yi_hbm, zi_hbm, mx_hbm, my_hbm, mz_hbm,
    v, xh, xp, xe, tab, gyz, cyz,
    xi, yi, zi, mx, my, mz, xcs, xc, wtab, sel, parts, zs1, zs2, zh, zp, z_rows, ytab, ztab, spread,
    load_sem, x1s, x1r, x2s, x2r, z1s, z1r, z2s, z2r, xcsem, xcrecv,
):
    gx, gy, gz = lax.axis_index("gx"), lax.axis_index("gy"), lax.axis_index("gz")
    nx, ny, nz = lax.axis_size("gx"), lax.axis_size("gy"), lax.axis_size("gz")
    me = gx * ny + gy
    count = nx * ny
    xl, xr = lax.rem(me + count - 1, count), lax.rem(me + 1, count)
    left = {"gx": xl // ny, "gy": lax.rem(xl, ny)}
    right = {"gx": xr // ny, "gy": lax.rem(xr, ny)}
    below = {"gz": lax.rem(gz + nz - 1, nz)}
    above = {"gz": lax.rem(gz + 1, nz)}
    barrier = pltpu.get_barrier_semaphore()
    for device in (left, right, below, above):
        pl.semaphore_signal(barrier, inc=1, device_id=device, device_id_type=MESH)

    loads = [
        pltpu.make_async_copy(src, dst, load_sem.at[k])
        for k, (src, dst) in enumerate(
            ((zi_hbm, zi), (xi_hbm, xi), (v_hbm, v), (yi_hbm, yi), (mx_hbm, mx), (my_hbm, my), (mz_hbm, mz)))
    ]
    for load in loads:
        load.start()
    cx, rows, cz = v.shape[1:]

    def send(src, dst, s, r, device):
        return pltpu.make_async_remote_copy(
            src_ref=src, dst_ref=dst, send_sem=s, recv_sem=r, device_id=device, device_id_type=MESH)

    step = rows // CHUNKS
    pl.semaphore_wait(barrier, 4)
    faces = []
    for c in range(CHUNKS):
        part = pl.ds(c * step, step)
        pair = (
            send(v_hbm.at[:, pl.ds(cx - 2, 2), part], xh.at[0, :, :, part], x1s.at[0, c], x1r.at[0, c], right),
            send(v_hbm.at[:, pl.ds(0, 2), part], xh.at[1, :, :, part], x1s.at[1, c], x1r.at[1, c], left),
        )
        for copy in pair:
            copy.start()
        faces.append(pair)

    loads[0].wait()
    z_inverse = zi[...]
    z_select(z_inverse, sel)
    corner = (z_inverse[0:1, 0:1], z_inverse[cz - 1 : cz, cz - 1 : cz])
    loads[1].wait()
    x_inverse = xi[...]
    xcs[0] = full(x_inverse[0:1, 0:1])
    xcs[1] = full(x_inverse[cx - 1 : cx, cx - 1 : cx])
    corners = (
        send(xcs.at[1], xc.at[0], xcsem.at[0], xcrecv.at[0], right),
        send(xcs.at[0], xc.at[1], xcsem.at[1], xcrecv.at[1], left),
    )
    for copy in corners:
        copy.start()
    loads[2].wait()
    pl.loop(0, cx)(lambda x: z_local(x, v, sel, corner, parts, zs1, zs2))
    z_faces = (
        send(zs1.at[1], zh.at[0], z1s.at[0], z1r.at[0], above),
        send(zs1.at[0], zh.at[1], z1s.at[1], z1r.at[1], below),
    )
    for copy in z_faces:
        copy.start()

    x_end_weights(x_inverse, wtab)
    pl.loop(0, rows // 8)(lambda t: x_local(t, v, wtab, xe))
    for load in loads[3:]:
        load.wait()
    ytab[...] = y_table(yi[...], my[...])

    for copy in z_faces:
        copy.wait()
    high, low = split(z_end_weights(z_inverse))
    wz = jnp.concatenate([high, high, low], axis=1)
    pl.loop(0, cx)(lambda x: z_halo(x, zh, wz, z_rows, zs2))
    z_ends = (
        send(zs2.at[1], zp.at[0], z2s.at[0], z2r.at[0], above),
        send(zs2.at[0], zp.at[1], z2s.at[1], z2r.at[1], below),
    )
    for copy in z_ends:
        copy.start()

    x_ends = []
    done = 0
    for c in range(CHUNKS):
        for copy in faces[c]:
            copy.wait()
        pl.loop(c * (step // 8), (c + 1) * (step // 8))(lambda t: x_halo(t, cx, xh, wtab, xe))
        part = pl.ds(c * step, step)
        pair = (
            send(xe.at[1, :, part], xp.at[0, :, part], x2s.at[0, c], x2r.at[0, c], right),
            send(xe.at[0, :, part], xp.at[1, :, part], x2s.at[1, c], x2r.at[1, c], left),
        )
        for copy in pair:
            copy.start()
        x_ends.append(pair)
        if c < CHUNKS - 1:
            pl.loop(done, done + BETWEEN)(lambda p: along_y(p, v, parts, ytab, gyz, cyz))
            done += BETWEEN

    pl.loop(done, cx // 2)(lambda p: along_y(p, v, parts, ytab, gyz, cyz))
    for copy in z_ends:
        copy.wait()
    for side in range(2):
        z_rows[:, 32 + 8 * side : 40 + 8 * side] = zp[side]
    z_tables(z_inverse, mz[...], zh[0, 0, 6:7, 0:1], zh[1, 0, 6:7, 0:1], ztab, spread)
    pl.loop(0, cx)(lambda x: along_z(x, parts, ztab, spread, z_rows, gyz, cyz))
    for copy in corners:
        copy.wait()
    x_tables(x_inverse, mx[...], xc, tab)
    for pair in x_ends:
        for copy in pair:
            copy.wait()


def exchange(velocity, x_inverse, y_inverse, z_inverse, metric_x, metric_y, metric_z):
    _, cx, rows, cz = velocity.shape
    dma = pltpu.SemaphoreType.DMA

    def vmem(*shape):
        return pltpu.VMEM(shape, F32)

    def half(*shape):
        return pltpu.VMEM(shape, BF16)

    outs = (
        (3, cx, rows, cz),
        (2, 3, 2, rows, cz),
        (2, 6, rows, cz),
        (2, 6, rows, cz),
        (3 * cx + 4, 8, 128),
        (2, 3, cx, rows, cz),
        (3, cx, rows, cz),
    )
    return pl.pallas_call(
        exchange_kernel,
        out_shape=tuple(jax.ShapeDtypeStruct(shape, F32) for shape in outs),
        in_specs=[pl.BlockSpec(memory_space=pltpu.HBM)] * 7,
        out_specs=(pl.BlockSpec(memory_space=pltpu.VMEM),) * len(outs),
        scratch_shapes=[
            vmem(cx, cx), vmem(rows, rows), vmem(cz, cz), vmem(1, cx), vmem(1, rows), vmem(1, cz),
            vmem(2, 8, 128), vmem(2, 8, 128), vmem(2 * (cx + 4), 8, 128),
            half(6, 64, 2 * cz), half(6, cx, rows, 2 * cz),
            vmem(2, cx, 8, rows), vmem(2, cx, 8, rows), vmem(2, cx, 8, rows), vmem(2, cx, 8, rows),
            vmem(cx, 64, rows),
            half(rows, 3 * rows), half(2 * cz, 2 * cz), half(192, 6 * cz),
            dma((7,)),
            dma((2, CHUNKS)), dma((2, CHUNKS)), dma((2, CHUNKS)), dma((2, CHUNKS)),
            dma((2,)), dma((2,)), dma((2,)), dma((2,)), dma((2,)), dma((2,)),
        ],
        compiler_params=pltpu.CompilerParams(
            collective_id=0, has_side_effects=True, vmem_limit_bytes=22 * MIB),
        name="exchange",
    )(*[
        pltpu.with_memory_space_constraint(a, pltpu.HBM)
        for a in (velocity, x_inverse, y_inverse, z_inverse, metric_x.reshape(1, cx),
                  metric_y.reshape(1, rows), metric_z.reshape(1, cz))
    ])


def x_sweep(part, v, xh, xp, xe, tab, gx, conv, cyz):
    cx = v.shape[1]

    def cell(j):
        if j < 0:
            velocity = [xh[0, i, j + 2, part] for i in range(3)]
        elif j >= cx:
            velocity = [xh[1, i, j - cx, part] for i in range(3)]
        else:
            velocity = [v[i, j, part] for i in range(3)]
        return velocity + [a * velocity[0] for a in velocity]

    window = [cell(j) for j in range(-2, 2)]
    state = None
    for j in range(cx):
        window.append(cell(j + 2))
        fresh = []
        for f in range(6):
            d = (window[3][f] - window[1][f]) + (FAR / NEAR) * (window[4][f] - window[0][f])
            for side, line in ((0, 0), (1, cx - 1)):
                if j == line:
                    k = 3 * cx + 2 * side
                    d = d - tab[k] * xp[side, f, part] + tab[k + 1] * xe[side, f, part]
            value = tab[j] * d
            if state is not None:
                value = value + tab[cx + j] * state[f]
            fresh.append(value)
            if j < cx - 1:
                if f < 3:
                    gx[f, j, part] = value
                else:
                    conv[f - 3, j, part] = value
        state = fresh
        window.pop(0)
    for j in range(cx - 1, -1, -1):
        if j < cx - 1:
            up = tab[2 * cx + j]
            state = [(gx[f, j, part] if f < 3 else conv[f - 3, j, part]) + up * state[f] for f in range(6)]
        for i in range(3):
            gx[i, j, part] = state[i]
            conv[i, j, part] = state[3 + i] + cyz[i, j, part]


def x_kernel(v, xh, xp, xe, tab, gyz, cyz, grad, conv, gx_out, conv_out, yz_sem, x_sem, c_sem):
    rows = v.shape[2]
    copies = [pltpu.make_async_copy(gyz.at[k], grad.at[:, 1 + k], yz_sem.at[k]) for k in range(2)]
    for copy in copies:
        copy.start()
    step = rows // OUT_CHUNKS
    for c in range(OUT_CHUNKS):
        @pl.loop(c * (step // 8), (c + 1) * (step // 8))
        def _(t):
            x_sweep(pl.ds(pl.multiple_of(t * 8, 8), 8), v, xh, xp, xe, tab, gx_out, conv_out, cyz)

        part = pl.ds(c * step, step)
        pair = (
            pltpu.make_async_copy(gx_out.at[:, :, part], grad.at[:, 0, :, part], x_sem.at[c]),
            pltpu.make_async_copy(conv_out.at[:, :, part], conv.at[:, :, part], c_sem.at[c]),
        )
        for copy in pair:
            copy.start()
        copies += pair
    for copy in copies:
        copy.wait()


def x_solve(v, xh, xp, xe, tab, gyz, cyz):
    _, cx, rows, cz = v.shape
    dma = pltpu.SemaphoreType.DMA
    return pl.pallas_call(
        x_kernel,
        out_shape=(
            jax.ShapeDtypeStruct((3, 3, cx, rows, cz), F32),
            jax.ShapeDtypeStruct((3, cx, rows, cz), F32),
        ),
        in_specs=[pl.BlockSpec(memory_space=pltpu.VMEM)] * 7,
        out_specs=(pl.BlockSpec(memory_space=pltpu.HBM),) * 2,
        scratch_shapes=[
            pltpu.VMEM((3, cx, rows, cz), F32),
            pltpu.VMEM((3, cx, rows, cz), F32),
            dma((2,)), dma((OUT_CHUNKS,)), dma((OUT_CHUNKS,)),
        ],
        compiler_params=pltpu.CompilerParams(vmem_limit_bytes=14 * MIB),
        name="x_solve",
    )(v, xh, xp, xe, tab, gyz, cyz)


def on_device(velocity, metric_x, metric_y, metric_z, x_inverse, y_inverse, z_inverse):
    return tuple(x_solve(*exchange(
        velocity, x_inverse, y_inverse, z_inverse, metric_x, metric_y, metric_z)))


def solution(mesh):
    return jax.shard_map(
        on_device,
        mesh=mesh,
        in_specs=(
            P(None, ("gx", "gy"), None, "gz"),
            P(("gx", "gy")),
            P(),
            P("gz"),
            P(("gx", "gy"), None),
            P(),
            P("gz", None),
        ),
        out_specs=(P(None, None, ("gx", "gy"), None, "gz"), P(None, ("gx", "gy"), None, "gz")),
        check_vma=False,
    )
```

```python
import jax
import jax.numpy as jnp
from jax import lax
from jax.experimental import pallas as pl
from jax.experimental.pallas import tpu as pltpu
from jax.sharding import PartitionSpec as P

COUPLING = 1.0 / 3.0
NEAR = 7.0 / 9.0
FAR = 1.0 / 36.0
F32 = jnp.float32
BF16 = jnp.bfloat16
MESH = pl.DeviceIdType.MESH
HIGH = lax.Precision.HIGHEST
CHUNKS = 2
OUT_CHUNKS = 6
MIB = 1 << 20


def split(values):
    high = values.astype(BF16)
    return high, (values - high.astype(F32)).astype(BF16)


def iota(shape, dim):
    return lax.broadcasted_iota(jnp.int32, shape, dim)


def band(size):
    step = iota((size, size), 1) - iota((size, size), 0)
    near = jnp.where(step == 1, NEAR, jnp.where(step == -1, -NEAR, 0.0))
    far = jnp.where(step == 2, FAR, jnp.where(step == -2, -FAR, 0.0))
    return (near + far).astype(F32)


def dot(a, b, dims=((1,), (0,)), precision=None):
    return lax.dot_general(a, b, (dims, ((), ())), precision=precision, preferred_element_type=F32)


def z_tables(z_inverse, metric, spread):
    size = z_inverse.shape[0]
    columns = z_inverse.T
    lines = [columns[k : k + 1] * metric for k in (0, 1, size - 2, size - 1)]
    row = iota((32, size), 0)
    zero = jnp.zeros((64, size), BF16)
    for field in range(6):
        table = jnp.zeros((32, size), F32)
        for k, line in enumerate(lines):
            table = jnp.where(row == 8 * k + field, line, table)
        high, low = split(table)
        spread[:, field * size : (field + 1) * size] = jnp.concatenate(
            [high, high, zero, low, low, zero], axis=0)


def z_weights(z_inverse, metric, weights):
    high, low = split(dot(z_inverse, band(z_inverse.shape[0]), precision=HIGH).T * metric)
    both = jnp.concatenate([high, low], axis=1)
    weights[...] = jnp.concatenate([both, both], axis=0)


def y_table(y_inverse, metric):
    size = y_inverse.shape[0]
    own = iota((size, size), 0) == iota((size, size), 1)
    column = jnp.sum(jnp.where(own, metric, 0.0), axis=1, keepdims=True)
    high, low = split(y_inverse)
    near, rest = split(band(size))
    product = dot(jnp.concatenate([high, low, high], axis=1), jnp.concatenate([near, near, rest], axis=0))
    high, low = split(product * column)
    return jnp.concatenate([high, high, low], axis=1)


def x_end_weights(inverse, store):
    size = inverse.shape[0]
    rows = size + 8
    step = iota((rows, size), 0) - iota((rows, size), 1) - 2
    near = jnp.where(step == 1, NEAR, jnp.where(step == -1, -NEAR, 0.0))
    far = jnp.where(step == 2, FAR, jnp.where(step == -2, -FAR, 0.0))
    taps = (near + far).astype(F32)
    for end, line in ((0, 0), (1, size - 1)):
        column = jnp.sum(taps * inverse[line : line + 1], axis=1, keepdims=True)
        store[end * rows : (end + 1) * rows] = jnp.broadcast_to(column, (rows, 128))


def x_tables(inverse, metric, corners, tab):
    size = inverse.shape[0]
    row, col = iota((size, size), 0), iota((size, size), 1)

    def pick(values, shift):
        return jnp.sum(jnp.where(col == row + shift, values, 0.0), axis=1, keepdims=True)

    def shifted(values, by):
        pad = jnp.zeros((1, values.shape[1]), F32)
        if by > 0:
            return jnp.concatenate([values[1:], pad], axis=0)
        return jnp.concatenate([pad, values[:-1]], axis=0)

    line = iota((size, 1), 0)
    below = shifted(inverse, 1)
    scale = pick(metric, 0)
    pivot = jnp.where(line < size - 1, pick(below, 1), 1.0)
    up = pick(inverse, 1) / pivot
    own = pick(inverse, 0) - up * pick(below, 0)
    before = jnp.where(line > 0, shifted(own, -1), 1.0)
    down = (pick(inverse, -1) - up * pick(below, -1)) / before
    above_scale = jnp.where(line < size - 1, pick(metric, 1), 1.0)
    below_scale = jnp.where(line > 0, pick(metric, -1), 1.0)
    for k, value in enumerate((NEAR * scale * own, down * scale / below_scale, up * scale / above_scale)):
        tab[k * size : (k + 1) * size] = jnp.broadcast_to(value, (size, 128))
    for side, end in ((0, 0), (1, size - 1)):
        own_end = inverse[end : end + 1, end : end + 1]
        other = corners[side]
        gain = (COUPLING / NEAR) / (1.0 - COUPLING * COUPLING * other * own_end)
        tab[3 * size + 16 * side : 3 * size + 16 * side + 8] = gain
        tab[3 * size + 16 * side + 8 : 3 * size + 16 * side + 16] = COUPLING * other * gain


def tile_of(table, row):
    return jnp.broadcast_to(table[row : row + 1], (8, 128))


def z_faces_of(v, corner, zs1):
    size, rows = v.shape[1:3]
    lane = iota((1, 128), 1)
    for k in range(2 * rows // 128):
        total = None
        for p in range(size // 2):
            for i in range(3):
                lines = v[i, 2 * p : 2 * p + 2].reshape(2 * rows, 128)[128 * k : 128 * k + 128]
                first = 16 * p + 4 * i
                moved = pltpu.roll(lines, first + 2, 1)
                total = moved if total is None else jnp.where((lane >= first) & (lane < first + 4), moved, total)
        got = total.T
        for p in range(size // 2):
            for side, layers in ((0, (2, 3)), (1, (0, 1))):
                lines = [got[16 * p + 4 * i + n : 16 * p + 4 * i + n + 1] for n in layers for i in range(3)]
                zs1[side, p, :, 128 * k : 128 * k + 128] = jnp.concatenate(
                    lines + [jnp.broadcast_to(corner[side], (1, 128)), jnp.zeros((1, 128), F32)], axis=0)


def z_ends_of(gather, inverse_metric, zs2):
    for k in range(gather.shape[0] // 128):
        got = gather[128 * k : 128 * k + 128].T
        for p in range(zs2.shape[1]):
            for side in range(2):
                lines = [got[16 * p + 2 * f + 1 - side : 16 * p + 2 * f + 2 - side] for f in range(6)]
                zs2[side, p, :, 128 * k : 128 * k + 128] = inverse_metric[side] * jnp.concatenate(
                    lines + [jnp.zeros((2, 128), F32)], axis=0)


def z_local(p, v, parts, ztab, gyz, cyz, gather):
    rows, cz = v.shape[2:]
    lane = iota((1, cz), 1)
    for k in range(2):
        x = 2 * p + k
        velocity = [v[i, x] for i in range(3)]
        for field in range(6):
            value = velocity[field] if field < 3 else velocity[field - 3] * velocity[2]
            parts[field, x] = jnp.concatenate(split(value), axis=1)
        got = dot(parts[:, x].reshape(6 * rows, 2 * cz), ztab[...])
        got = got[:, :cz] + got[:, cz:]
        ends = gather[k * rows : (k + 1) * rows]
        for f in range(6):
            values = got[f * rows : (f + 1) * rows]
            if f < 3:
                gyz[1, f, x] = values
            else:
                cyz[f - 3, x] = values
            first = 16 * p + 2 * f
            ends = jnp.where((lane >= first) & (lane < first + 2), pltpu.roll(values, first + 1, 1), ends)
        gather[k * rows : (k + 1) * rows] = ends


def beside(halo, near, far):
    def six(first):
        lines = halo[first : first + 3]
        pad = jnp.zeros((2, lines.shape[1]), F32)
        return jnp.concatenate([lines, lines * lines[2:3], pad], axis=0)

    return six(near), six(far)


def z_halo(zh, z_inverse, zs2):
    size = z_inverse.shape[0]
    weights = []
    for line in (0, size - 1):
        a, b, c, d = (z_inverse[line : line + 1, k : k + 1] for k in (0, 1, size - 2, size - 1))
        weights.append((-NEAR * a - FAR * b, -FAR * a, NEAR * d + FAR * c, FAR * d))
    for p in range(zh.shape[1]):
        layers = beside(zh[0, p], 3, 0) + beside(zh[1, p], 0, 3)
        for side in range(2):
            total = zs2[side, p]
            for weight, layer in zip(weights[side], layers):
                total = total + weight * layer
            zs2[side, p] = total


def z_correct(q, spread, z_inverse, zh, zp, zs2, gyz, cyz):
    rows, cz = gyz.shape[3:]
    square = COUPLING * COUPLING
    own = (z_inverse[0:1, 0:1], z_inverse[cz - 1 : cz, cz - 1 : cz])
    lines = []
    for k in range(2):
        p = 2 * q + k
        terms = []
        for side, sign in ((0, -1.0), (1, 1.0)):
            halo = zh[side, p]
            near, far = beside(halo, 3 - 3 * side, 3 * side)
            other = halo[6:7, 0:1]
            gain = COUPLING / (1.0 - square * other * own[side])
            first = (sign * NEAR) * near + (sign * FAR) * far - gain * zp[side, p]
            first = first + (COUPLING * other * gain) * zs2[side, p]
            second = (sign * FAR) * near
            terms += [first, second] if side == 0 else [second, first]
        high, low = split(jnp.concatenate(terms, axis=0))
        lines += [high.astype(F32), low.astype(F32)]
    turned = jnp.concatenate(lines, axis=0).T
    turned = jnp.concatenate([turned, pltpu.roll(turned, 64, 1)], axis=0).astype(BF16)
    more = dot(jnp.concatenate([turned, turned], axis=1), spread[...])
    planes = pl.ds(4 * q, 4)
    for i in range(3):
        gyz[1, i, planes] = gyz[1, i, planes] + more[:, i * cz : (i + 1) * cz].reshape(4, rows, cz)
        cyz[i, planes] = cyz[i, planes] + more[:, (3 + i) * cz : (4 + i) * cz].reshape(4, rows, cz)


def x_local(t, v, wtab, xe):
    part = pl.ds(pl.multiple_of(t * 8, 8), 8)
    size = v.shape[1]
    ends = [[None] * 6, [None] * 6]
    for j in range(size):
        velocity = [v[i, j, part] for i in range(3)]
        fields = velocity + [a * velocity[0] for a in velocity]
        for end in range(2):
            weight = tile_of(wtab, end * (size + 8) + j + 2)
            for f in range(6):
                term = weight * fields[f]
                ends[end][f] = term if ends[end][f] is None else ends[end][f] + term
    for end in range(2):
        for f in range(6):
            xe[end, f, part] = ends[end][f]


def x_halo(t, size, xh, wtab, xe):
    part = pl.ds(pl.multiple_of(t * 8, 8), 8)
    ends = [[xe[end, f, part] for f in range(6)] for end in range(2)]
    for side in range(2):
        for layer in range(2):
            j = layer - 2 if side == 0 else size + layer
            velocity = [xh[side, i, layer, part] for i in range(3)]
            fields = velocity + [a * velocity[0] for a in velocity]
            for end in range(2):
                weight = tile_of(wtab, end * (size + 8) + j + 2)
                for f in range(6):
                    ends[end][f] = ends[end][f] + weight * fields[f]
    for end in range(2):
        for f in range(6):
            xe[end, f, part] = ends[end][f]


def along_y(p, v, parts, ytab, gyz, cyz):
    cz = v.shape[3]
    planes = (2 * p, 2 * p + 1)

    def apply(pieces):
        high = jnp.concatenate([a[0] for a in pieces], axis=1)
        low = jnp.concatenate([a[1] for a in pieces], axis=1)
        return dot(ytab[...], jnp.concatenate([high, low, high], axis=0))

    def held(field):
        got = [parts[field, x] for x in planes]
        return [(g[:, :cz], g[:, cz:]) for g in got]

    for i in range(3):
        got = apply(held(i))
        for k, x in enumerate(planes):
            gyz[0, i, x] = got[:, k * cz : (k + 1) * cz]
        got = apply(held(4) if i == 2 else [split(v[i, x] * v[1, x]) for x in planes])
        for k, x in enumerate(planes):
            cyz[i, x] = cyz[i, x] + got[:, k * cz : (k + 1) * cz]


def exchange_kernel(
    v_hbm, xi_hbm, yi_hbm, zi_hbm, mx_hbm, my_hbm, mz_hbm,
    v, xh, xp, xe, tab, gyz, cyz,
    xi, yi, zi, mx, my, mz, xcs, xc, wtab, parts, zs1, zs2, zh, zp, gather, ytab, ztab, spread,
    load_sem, x1s, x1r, x2s, x2r, z1s, z1r, z2s, z2r, xcsem, xcrecv,
):
    gx, gy, gz = lax.axis_index("gx"), lax.axis_index("gy"), lax.axis_index("gz")
    nx, ny, nz = lax.axis_size("gx"), lax.axis_size("gy"), lax.axis_size("gz")
    me = gx * ny + gy
    count = nx * ny
    xl, xr = lax.rem(me + count - 1, count), lax.rem(me + 1, count)
    left = {"gx": xl // ny, "gy": lax.rem(xl, ny)}
    right = {"gx": xr // ny, "gy": lax.rem(xr, ny)}
    below = {"gz": lax.rem(gz + nz - 1, nz)}
    above = {"gz": lax.rem(gz + 1, nz)}
    barrier = pltpu.get_barrier_semaphore()
    for device in (left, right, below, above):
        pl.semaphore_signal(barrier, inc=1, device_id=device, device_id_type=MESH)

    loads = [
        pltpu.make_async_copy(src, dst, load_sem.at[k])
        for k, (src, dst) in enumerate(
            ((zi_hbm, zi), (xi_hbm, xi), (v_hbm, v), (yi_hbm, yi), (mx_hbm, mx), (my_hbm, my), (mz_hbm, mz)))
    ]
    for load in loads:
        load.start()
    cx, rows, cz = v.shape[1:]

    def send(src, dst, s, r, device):
        return pltpu.make_async_remote_copy(
            src_ref=src, dst_ref=dst, send_sem=s, recv_sem=r, device_id=device, device_id_type=MESH)

    step = rows // CHUNKS
    pl.semaphore_wait(barrier, 4)
    faces = []
    for c in range(CHUNKS):
        part = pl.ds(c * step, step)
        pair = (
            send(v_hbm.at[:, pl.ds(cx - 2, 2), part], xh.at[0, :, :, part], x1s.at[0, c], x1r.at[0, c], right),
            send(v_hbm.at[:, pl.ds(0, 2), part], xh.at[1, :, :, part], x1s.at[1, c], x1r.at[1, c], left),
        )
        for copy in pair:
            copy.start()
        faces.append(pair)

    loads[0].wait()
    loads[6].wait()
    z_inverse = zi[...]
    corner = (z_inverse[0:1, 0:1], z_inverse[cz - 1 : cz, cz - 1 : cz])
    z_weights(z_inverse, mz[...], ztab)
    loads[1].wait()
    x_inverse = xi[...]
    xcs[0] = jnp.broadcast_to(x_inverse[0:1, 0:1], (8, 128))
    xcs[1] = jnp.broadcast_to(x_inverse[cx - 1 : cx, cx - 1 : cx], (8, 128))
    corners = (
        send(xcs.at[1], xc.at[0], xcsem.at[0], xcrecv.at[0], right),
        send(xcs.at[0], xc.at[1], xcsem.at[1], xcrecv.at[1], left),
    )
    for copy in corners:
        copy.start()
    loads[2].wait()
    z_faces_of(v, corner, zs1)
    z_faces = (
        send(zs1.at[1], zh.at[0], z1s.at[0], z1r.at[0], above),
        send(zs1.at[0], zh.at[1], z1s.at[1], z1r.at[1], below),
    )
    for copy in z_faces:
        copy.start()

    x_end_weights(x_inverse, wtab)
    pl.loop(0, rows // 8)(lambda t: x_local(t, v, wtab, xe))
    inverse_metric = (1.0 / mz[:, 0:1], 1.0 / mz[:, cz - 1 : cz])

    def z_pass(first, last):
        pl.loop(first, last)(lambda p: z_local(p, v, parts, ztab, gyz, cyz, gather))

    x_ends = []

    def x_pass(c):
        for copy in faces[c]:
            copy.wait()
        pl.loop(c * (step // 8), (c + 1) * (step // 8))(lambda t: x_halo(t, cx, xh, wtab, xe))
        part = pl.ds(c * step, step)
        pair = (
            send(xe.at[1, :, part], xp.at[0, :, part], x2s.at[0, c], x2r.at[0, c], right),
            send(xe.at[0, :, part], xp.at[1, :, part], x2s.at[1, c], x2r.at[1, c], left),
        )
        for copy in pair:
            copy.start()
        x_ends.append(pair)

    z_tables(z_inverse, mz[...], spread)
    gather[...] = jnp.zeros(gather.shape, F32)
    z_pass(0, cx // 4)
    x_pass(0)
    z_pass(cx // 4, cx // 2)
    for copy in z_faces:
        copy.wait()
    z_ends_of(gather, inverse_metric, zs2)
    z_halo(zh, z_inverse, zs2)
    z_ends = (
        send(zs2.at[1], zp.at[0], z2s.at[0], z2r.at[0], above),
        send(zs2.at[0], zp.at[1], z2s.at[1], z2r.at[1], below),
    )
    for copy in z_ends:
        copy.start()
    for c in range(1, CHUNKS):
        x_pass(c)

    for load in loads[3:6]:
        load.wait()
    ytab[...] = y_table(yi[...], my[...])
    pl.loop(0, cx // 2)(lambda p: along_y(p, v, parts, ytab, gyz, cyz))
    for copy in z_ends:
        copy.wait()
    pl.loop(0, cx // 4)(lambda q: z_correct(q, spread, z_inverse, zh, zp, zs2, gyz, cyz))
    for copy in corners:
        copy.wait()
    x_tables(x_inverse, mx[...], xc, tab)
    for pair in x_ends:
        for copy in pair:
            copy.wait()


def exchange(velocity, x_inverse, y_inverse, z_inverse, metric_x, metric_y, metric_z):
    _, cx, rows, cz = velocity.shape
    dma = pltpu.SemaphoreType.DMA

    def vmem(*shape):
        return pltpu.VMEM(shape, F32)

    def half(*shape):
        return pltpu.VMEM(shape, BF16)

    outs = (
        (3, cx, rows, cz),
        (2, 3, 2, rows, cz),
        (2, 6, rows, cz),
        (2, 6, rows, cz),
        (3 * cx + 32, 128),
        (2, 3, cx, rows, cz),
        (3, cx, rows, cz),
    )
    return pl.pallas_call(
        exchange_kernel,
        out_shape=tuple(jax.ShapeDtypeStruct(shape, F32) for shape in outs),
        in_specs=[pl.BlockSpec(memory_space=pltpu.HBM)] * 7,
        out_specs=(pl.BlockSpec(memory_space=pltpu.VMEM),) * len(outs),
        scratch_shapes=[
            vmem(cx, cx), vmem(rows, rows), vmem(cz, cz), vmem(1, cx), vmem(1, rows), vmem(1, cz),
            vmem(2, 8, 128), vmem(2, 8, 128), vmem(2 * (cx + 8), 128),
            half(6, cx, rows, 2 * cz),
            *[vmem(2, cx // 2, 8, 2 * rows)] * 4, vmem(2 * rows, cz),
            half(rows, 3 * rows), half(2 * cz, 2 * cz), half(256, 6 * cz),
            dma((7,)),
            dma((2, CHUNKS)), dma((2, CHUNKS)), dma((2, CHUNKS)), dma((2, CHUNKS)),
            dma((2,)), dma((2,)), dma((2,)), dma((2,)), dma((2,)), dma((2,)),
        ],
        compiler_params=pltpu.CompilerParams(
            collective_id=0, has_side_effects=True, vmem_limit_bytes=22 * MIB),
        name="exchange",
    )(*[
        pltpu.with_memory_space_constraint(a, pltpu.HBM)
        for a in (velocity, x_inverse, y_inverse, z_inverse, metric_x.reshape(1, cx),
                  metric_y.reshape(1, rows), metric_z.reshape(1, cz))
    ])


def x_sweep(part, v, xh, xp, xe, tab, gx, conv, cyz):
    cx = v.shape[1]

    def cell(j):
        if j < 0:
            velocity = [xh[0, i, j + 2, part] for i in range(3)]
        elif j >= cx:
            velocity = [xh[1, i, j - cx, part] for i in range(3)]
        else:
            velocity = [v[i, j, part] for i in range(3)]
        return velocity + [a * velocity[0] for a in velocity]

    window = [cell(j) for j in range(-2, 2)]
    state = None
    for j in range(cx):
        window.append(cell(j + 2))
        fresh = []
        for f in range(6):
            d = (window[3][f] - window[1][f]) + (FAR / NEAR) * (window[4][f] - window[0][f])
            for side, line in ((0, 0), (1, cx - 1)):
                if j == line:
                    k = 3 * cx + 16 * side
                    d = d - tab[k : k + 8] * xp[side, f, part] + tab[k + 8 : k + 16] * xe[side, f, part]
            value = tile_of(tab, j) * d
            if state is not None:
                value = value + tile_of(tab, cx + j) * state[f]
            fresh.append(value)
            if j < cx - 1:
                if f < 3:
                    gx[f, j, part] = value
                else:
                    conv[f - 3, j, part] = value
        state = fresh
        window.pop(0)
    for j in range(cx - 1, -1, -1):
        if j < cx - 1:
            up = tile_of(tab, 2 * cx + j)
            state = [(gx[f, j, part] if f < 3 else conv[f - 3, j, part]) + up * state[f] for f in range(6)]
        for i in range(3):
            gx[i, j, part] = state[i]
            conv[i, j, part] = state[3 + i] + cyz[i, j, part]


def x_kernel(v, xh, xp, xe, tab, gyz, cyz, grad, conv, gx_out, conv_out, yz_sem, x_sem, c_sem):
    rows = v.shape[2]
    copies = [pltpu.make_async_copy(gyz.at[k], grad.at[:, 1 + k], yz_sem.at[k]) for k in range(2)]
    for copy in copies:
        copy.start()
    step = rows // OUT_CHUNKS
    for c in range(OUT_CHUNKS):
        @pl.loop(c * (step // 8), (c + 1) * (step // 8))
        def _(t):
            x_sweep(pl.ds(pl.multiple_of(t * 8, 8), 8), v, xh, xp, xe, tab, gx_out, conv_out, cyz)

        part = pl.ds(c * step, step)
        pair = (
            pltpu.make_async_copy(gx_out.at[:, :, part], grad.at[:, 0, :, part], x_sem.at[c]),
            pltpu.make_async_copy(conv_out.at[:, :, part], conv.at[:, :, part], c_sem.at[c]),
        )
        for copy in pair:
            copy.start()
        copies += pair
    for copy in copies:
        copy.wait()


def x_solve(v, xh, xp, xe, tab, gyz, cyz):
    _, cx, rows, cz = v.shape
    dma = pltpu.SemaphoreType.DMA
    return pl.pallas_call(
        x_kernel,
        out_shape=(
            jax.ShapeDtypeStruct((3, 3, cx, rows, cz), F32),
            jax.ShapeDtypeStruct((3, cx, rows, cz), F32),
        ),
        in_specs=[pl.BlockSpec(memory_space=pltpu.VMEM)] * 7,
        out_specs=(pl.BlockSpec(memory_space=pltpu.HBM),) * 2,
        scratch_shapes=[
            pltpu.VMEM((3, cx, rows, cz), F32),
            pltpu.VMEM((3, cx, rows, cz), F32),
            dma((2,)), dma((OUT_CHUNKS,)), dma((OUT_CHUNKS,)),
        ],
        compiler_params=pltpu.CompilerParams(vmem_limit_bytes=14 * MIB),
        name="x_solve",
    )(v, xh, xp, xe, tab, gyz, cyz)


def on_device(velocity, metric_x, metric_y, metric_z, x_inverse, y_inverse, z_inverse):
    return tuple(x_solve(*exchange(
        velocity, x_inverse, y_inverse, z_inverse, metric_x, metric_y, metric_z)))


def solution(mesh):
    return jax.shard_map(
        on_device,
        mesh=mesh,
        in_specs=(
            P(None, ("gx", "gy"), None, "gz"),
            P(("gx", "gy")),
            P(),
            P("gz"),
            P(("gx", "gy"), None),
            P(),
            P("gz", None),
        ),
        out_specs=(P(None, None, ("gx", "gy"), None, "gz"), P(None, ("gx", "gy"), None, "gz")),
        check_vma=False,
    )
```

```python
import jax
import jax.numpy as jnp
from jax import lax
from jax.experimental import pallas as pl
from jax.experimental.pallas import tpu as pltpu
from jax.sharding import PartitionSpec as P

COUPLING = 1.0 / 3.0
NEAR = 7.0 / 9.0
FAR = 1.0 / 36.0
F32 = jnp.float32
BF16 = jnp.bfloat16
MESH = pl.DeviceIdType.MESH
HIGH = lax.Precision.HIGHEST
CHUNKS = 2
OUT_CHUNKS = 6
PLANES = 8
EARLY = True
MIB = 1 << 20


def split(values):
    high = values.astype(BF16)
    return high, (values - high.astype(F32)).astype(BF16)


def iota(shape, dim):
    return lax.broadcasted_iota(jnp.int32, shape, dim)


def band(size):
    step = iota((size, size), 1) - iota((size, size), 0)
    near = jnp.where(step == 1, NEAR, jnp.where(step == -1, -NEAR, 0.0))
    far = jnp.where(step == 2, FAR, jnp.where(step == -2, -FAR, 0.0))
    return (near + far).astype(F32)


def dot(a, b, dims=((1,), (0,)), precision=None):
    return lax.dot_general(a, b, (dims, ((), ())), precision=precision, preferred_element_type=F32)


def z_tables(z_inverse, metric, spread):
    size = z_inverse.shape[0]
    columns = z_inverse.T
    lines = [columns[k : k + 1] * metric for k in (0, 1, size - 2, size - 1)]
    row = iota((32, size), 0)
    zero = jnp.zeros((64, size), BF16)
    for field in range(6):
        table = jnp.zeros((32, size), F32)
        for k, line in enumerate(lines):
            table = jnp.where(row == 8 * k + field, line, table)
        high, low = split(table)
        spread[:, field * size : (field + 1) * size] = jnp.concatenate(
            [high, high, zero, low, low, zero], axis=0)


def z_weights(z_inverse, metric, weights):
    high, low = split(dot(z_inverse, band(z_inverse.shape[0]), precision=HIGH).T * metric)
    both = jnp.concatenate([high, low], axis=1)
    weights[...] = jnp.concatenate([both, both], axis=0)


def y_table(y_inverse, metric):
    size = y_inverse.shape[0]
    own = iota((size, size), 0) == iota((size, size), 1)
    column = jnp.sum(jnp.where(own, metric, 0.0), axis=1, keepdims=True)
    high, low = split(y_inverse)
    near, rest = split(band(size))
    product = dot(jnp.concatenate([high, low, high], axis=1), jnp.concatenate([near, near, rest], axis=0))
    high, low = split(product * column)
    return jnp.concatenate([high, high, low], axis=1)


def x_end_weights(inverse, store):
    size = inverse.shape[0]
    rows = size + 8
    step = iota((rows, size), 0) - iota((rows, size), 1) - 2
    near = jnp.where(step == 1, NEAR, jnp.where(step == -1, -NEAR, 0.0))
    far = jnp.where(step == 2, FAR, jnp.where(step == -2, -FAR, 0.0))
    taps = (near + far).astype(F32)
    for end, line in ((0, 0), (1, size - 1)):
        column = jnp.sum(taps * inverse[line : line + 1], axis=1, keepdims=True)
        store[end * rows : (end + 1) * rows] = jnp.broadcast_to(column, (rows, 128))


def x_tables(inverse, metric, corners, tab):
    size = inverse.shape[0]
    row, col = iota((size, size), 0), iota((size, size), 1)

    def pick(values, shift):
        return jnp.sum(jnp.where(col == row + shift, values, 0.0), axis=1, keepdims=True)

    def shifted(values, by):
        pad = jnp.zeros((1, values.shape[1]), F32)
        if by > 0:
            return jnp.concatenate([values[1:], pad], axis=0)
        return jnp.concatenate([pad, values[:-1]], axis=0)

    line = iota((size, 1), 0)
    below = shifted(inverse, 1)
    scale = pick(metric, 0)
    pivot = jnp.where(line < size - 1, pick(below, 1), 1.0)
    up = pick(inverse, 1) / pivot
    own = pick(inverse, 0) - up * pick(below, 0)
    before = jnp.where(line > 0, shifted(own, -1), 1.0)
    down = (pick(inverse, -1) - up * pick(below, -1)) / before
    above_scale = jnp.where(line < size - 1, pick(metric, 1), 1.0)
    below_scale = jnp.where(line > 0, pick(metric, -1), 1.0)
    for k, value in enumerate((NEAR * scale * own, down * scale / below_scale, up * scale / above_scale)):
        tab[k * size : (k + 1) * size] = jnp.broadcast_to(value, (size, 128))
    for side, end in ((0, 0), (1, size - 1)):
        own_end = inverse[end : end + 1, end : end + 1]
        other = corners[side]
        gain = (COUPLING / NEAR) / (1.0 - COUPLING * COUPLING * other * own_end)
        tab[3 * size + 16 * side : 3 * size + 16 * side + 8] = gain
        tab[3 * size + 16 * side + 8 : 3 * size + 16 * side + 16] = COUPLING * other * gain


def tile_of(table, row):
    return jnp.broadcast_to(table[row : row + 1], (8, 128))


def z_faces_of(v, corner, zs1):
    size, rows = v.shape[1:3]
    lane = iota((1, 128), 1)
    for k in range(2 * rows // 128):
        total = None
        for p in range(size // 2):
            for i in range(3):
                lines = v[i, 2 * p : 2 * p + 2].reshape(2 * rows, 128)[128 * k : 128 * k + 128]
                first = 16 * p + 4 * i
                moved = pltpu.roll(lines, first + 2, 1)
                total = moved if total is None else jnp.where((lane >= first) & (lane < first + 4), moved, total)
        got = total.T
        for p in range(size // 2):
            for side, layers in ((0, (2, 3)), (1, (0, 1))):
                lines = [got[16 * p + 4 * i + n : 16 * p + 4 * i + n + 1] for n in layers for i in range(3)]
                zs1[side, p, :, 128 * k : 128 * k + 128] = jnp.concatenate(
                    lines + [jnp.broadcast_to(corner[side], (1, 128)), jnp.zeros((1, 128), F32)], axis=0)


def z_ends_of(gather, inverse_metric, zs2):
    for k in range(gather.shape[0] // 128):
        got = gather[128 * k : 128 * k + 128].T
        for p in range(zs2.shape[1]):
            for side in range(2):
                lines = [got[16 * p + 2 * f + 1 - side : 16 * p + 2 * f + 2 - side] for f in range(6)]
                zs2[side, p, :, 128 * k : 128 * k + 128] = inverse_metric[side] * jnp.concatenate(
                    lines + [jnp.zeros((2, 128), F32)], axis=0)


def z_local(q, v, parts, ztab, gyz, cyz, gather):
    rows, cz = v.shape[2:]
    lane = iota((1, cz), 1)
    planes = [PLANES * q + k for k in range(PLANES)]
    for x in planes:
        velocity = [v[i, x] for i in range(3)]
        for field in range(6):
            value = velocity[field] if field < 3 else velocity[field - 3] * velocity[2]
            parts[field, x] = jnp.concatenate(split(value), axis=1)
    ends = [gather[k * rows : (k + 1) * rows] for k in range(2)]
    for k, x in enumerate(planes):
        got = dot(parts[:, x].reshape(6 * rows, 2 * cz), ztab[...])
        got = got[:, :cz] + got[:, cz:]
        for f in range(6):
            values = got[f * rows : (f + 1) * rows]
            if f < 3:
                gyz[1, f, x] = values
            else:
                cyz[f - 3, x] = values
            first = 8 * PLANES * q + 16 * (k // 2) + 2 * f
            kept = (lane >= first) & (lane < first + 2)
            ends[k % 2] = jnp.where(kept, pltpu.roll(values, first + 1, 1), ends[k % 2])
    for k in range(2):
        gather[k * rows : (k + 1) * rows] = ends[k]


def beside(halo, near, far):
    def six(first):
        lines = halo[first : first + 3]
        pad = jnp.zeros((2, lines.shape[1]), F32)
        return jnp.concatenate([lines, lines * lines[2:3], pad], axis=0)

    return six(near), six(far)


def z_halo(zh, z_inverse, zs2):
    size = z_inverse.shape[0]
    weights = []
    for line in (0, size - 1):
        a, b, c, d = (z_inverse[line : line + 1, k : k + 1] for k in (0, 1, size - 2, size - 1))
        weights.append((-NEAR * a - FAR * b, -FAR * a, NEAR * d + FAR * c, FAR * d))
    for p in range(zh.shape[1]):
        layers = beside(zh[0, p], 3, 0) + beside(zh[1, p], 0, 3)
        for side in range(2):
            total = zs2[side, p]
            for weight, layer in zip(weights[side], layers):
                total = total + weight * layer
            zs2[side, p] = total


def z_correct(q, spread, z_inverse, zh, zp, zs2, gyz, cyz):
    rows, cz = gyz.shape[3:]
    square = COUPLING * COUPLING
    own = (z_inverse[0:1, 0:1], z_inverse[cz - 1 : cz, cz - 1 : cz])
    lines = []
    for k in range(2):
        p = 2 * q + k
        terms = []
        for side, sign in ((0, -1.0), (1, 1.0)):
            halo = zh[side, p]
            near, far = beside(halo, 3 - 3 * side, 3 * side)
            other = halo[6:7, 0:1]
            gain = COUPLING / (1.0 - square * other * own[side])
            first = (sign * NEAR) * near + (sign * FAR) * far - gain * zp[side, p]
            first = first + (COUPLING * other * gain) * zs2[side, p]
            second = (sign * FAR) * near
            terms += [first, second] if side == 0 else [second, first]
        high, low = split(jnp.concatenate(terms, axis=0))
        lines += [high.astype(F32), low.astype(F32)]
    turned = jnp.concatenate(lines, axis=0).T
    turned = jnp.concatenate([turned, pltpu.roll(turned, 64, 1)], axis=0).astype(BF16)
    more = dot(jnp.concatenate([turned, turned], axis=1), spread[...])
    planes = pl.ds(4 * q, 4)
    for i in range(3):
        gyz[1, i, planes] = gyz[1, i, planes] + more[:, i * cz : (i + 1) * cz].reshape(4, rows, cz)
        cyz[i, planes] = cyz[i, planes] + more[:, (3 + i) * cz : (4 + i) * cz].reshape(4, rows, cz)


def x_local(t, v, wtab, xe):
    part = pl.ds(pl.multiple_of(t * 8, 8), 8)
    size = v.shape[1]
    ends = [[None] * 6, [None] * 6]
    for j in range(size):
        velocity = [v[i, j, part] for i in range(3)]
        fields = velocity + [a * velocity[0] for a in velocity]
        for end in range(2):
            weight = tile_of(wtab, end * (size + 8) + j + 2)
            for f in range(6):
                term = weight * fields[f]
                ends[end][f] = term if ends[end][f] is None else ends[end][f] + term
    for end in range(2):
        for f in range(6):
            xe[end, f, part] = ends[end][f]


def x_halo(t, size, xh, wtab, xe):
    part = pl.ds(pl.multiple_of(t * 8, 8), 8)
    ends = [[xe[end, f, part] for f in range(6)] for end in range(2)]
    for side in range(2):
        for layer in range(2):
            j = layer - 2 if side == 0 else size + layer
            velocity = [xh[side, i, layer, part] for i in range(3)]
            fields = velocity + [a * velocity[0] for a in velocity]
            for end in range(2):
                weight = tile_of(wtab, end * (size + 8) + j + 2)
                for f in range(6):
                    ends[end][f] = ends[end][f] + weight * fields[f]
    for end in range(2):
        for f in range(6):
            xe[end, f, part] = ends[end][f]


def along_y(q, v, parts, ytab, gyz, cyz):
    cz = v.shape[3]
    planes = [PLANES * q + k for k in range(PLANES)]

    def apply(pieces):
        high = jnp.concatenate([a[0] for a in pieces], axis=1)
        low = jnp.concatenate([a[1] for a in pieces], axis=1)
        return dot(ytab[...], jnp.concatenate([high, low, high], axis=0))

    def held(field):
        got = [parts[field, x] for x in planes]
        return [(g[:, :cz], g[:, cz:]) for g in got]

    for i in range(3):
        got = apply(held(i))
        for k, x in enumerate(planes):
            gyz[0, i, x] = got[:, k * cz : (k + 1) * cz]
        got = apply(held(4) if i == 2 else [split(v[i, x] * v[1, x]) for x in planes])
        for k, x in enumerate(planes):
            cyz[i, x] = cyz[i, x] + got[:, k * cz : (k + 1) * cz]


def times(body, start, stop, unit):
    @pl.loop(start // unit, stop // unit)
    def _(t):
        for k in range(unit):
            body(unit * t + k)


def exchange_kernel(
    v_hbm, xi_hbm, yi_hbm, zi_hbm, mx_hbm, my_hbm, mz_hbm,
    v, xh, xp, xe, tab, gyz, cyz,
    xi, yi, zi, mx, my, mz, xcs, xc, wtab, parts, zs1, zs2, zh, zp, gather, ytab, ztab, spread,
    load_sem, x1s, x1r, x2s, x2r, z1s, z1r, z2s, z2r, xcsem, xcrecv,
):
    gx, gy, gz = lax.axis_index("gx"), lax.axis_index("gy"), lax.axis_index("gz")
    nx, ny, nz = lax.axis_size("gx"), lax.axis_size("gy"), lax.axis_size("gz")
    me = gx * ny + gy
    count = nx * ny
    xl, xr = lax.rem(me + count - 1, count), lax.rem(me + 1, count)
    left = {"gx": xl // ny, "gy": lax.rem(xl, ny)}
    right = {"gx": xr // ny, "gy": lax.rem(xr, ny)}
    below = {"gz": lax.rem(gz + nz - 1, nz)}
    above = {"gz": lax.rem(gz + 1, nz)}
    barrier = pltpu.get_barrier_semaphore()
    for device in (left, right, below, above):
        pl.semaphore_signal(barrier, inc=1, device_id=device, device_id_type=MESH)

    loads = [
        pltpu.make_async_copy(src, dst, load_sem.at[k])
        for k, (src, dst) in enumerate(
            ((zi_hbm, zi), (xi_hbm, xi), (v_hbm, v), (yi_hbm, yi), (mx_hbm, mx), (my_hbm, my), (mz_hbm, mz)))
    ]
    for load in loads:
        load.start()
    cx, rows, cz = v.shape[1:]

    def send(src, dst, s, r, device):
        return pltpu.make_async_remote_copy(
            src_ref=src, dst_ref=dst, send_sem=s, recv_sem=r, device_id=device, device_id_type=MESH)

    step = rows // CHUNKS
    loads[0].wait()
    loads[1].wait()
    loads[6].wait()
    z_inverse = zi[...]
    corner = (z_inverse[0:1, 0:1], z_inverse[cz - 1 : cz, cz - 1 : cz])
    z_weights(z_inverse, mz[...], ztab)
    x_inverse = xi[...]
    xcs[0] = jnp.broadcast_to(x_inverse[0:1, 0:1], (8, 128))
    xcs[1] = jnp.broadcast_to(x_inverse[cx - 1 : cx, cx - 1 : cx], (8, 128))
    x_end_weights(x_inverse, wtab)
    loads[2].wait()
    z_faces_of(v, corner, zs1)
    if EARLY:
        times(lambda t: x_local(t, v, wtab, xe), 0, rows // 8, 2)

    pl.semaphore_wait(barrier, 4)
    faces = []
    for c in range(CHUNKS):
        part = pl.ds(c * step, step)
        pair = (
            send(v.at[:, pl.ds(cx - 2, 2), part], xh.at[0, :, :, part], x1s.at[0, c], x1r.at[0, c], right),
            send(v.at[:, pl.ds(0, 2), part], xh.at[1, :, :, part], x1s.at[1, c], x1r.at[1, c], left),
        )
        for copy in pair:
            copy.start()
        faces.append(pair)
    corners = (
        send(xcs.at[1], xc.at[0], xcsem.at[0], xcrecv.at[0], right),
        send(xcs.at[0], xc.at[1], xcsem.at[1], xcrecv.at[1], left),
    )
    for copy in corners:
        copy.start()
    z_faces = (
        send(zs1.at[1], zh.at[0], z1s.at[0], z1r.at[0], above),
        send(zs1.at[0], zh.at[1], z1s.at[1], z1r.at[1], below),
    )
    for copy in z_faces:
        copy.start()
    if not EARLY:
        times(lambda t: x_local(t, v, wtab, xe), 0, rows // 8, 2)

    inverse_metric = (1.0 / mz[:, 0:1], 1.0 / mz[:, cz - 1 : cz])

    def z_pass(first, last):
        pl.loop(first, last)(lambda p: z_local(p, v, parts, ztab, gyz, cyz, gather))

    x_ends = []

    def x_pass(c):
        for copy in faces[c]:
            copy.wait()
        times(lambda t: x_halo(t, cx, xh, wtab, xe), c * (step // 8), (c + 1) * (step // 8), 2)
        part = pl.ds(c * step, step)
        pair = (
            send(xe.at[1, :, part], xp.at[0, :, part], x2s.at[0, c], x2r.at[0, c], right),
            send(xe.at[0, :, part], xp.at[1, :, part], x2s.at[1, c], x2r.at[1, c], left),
        )
        for copy in pair:
            copy.start()
        x_ends.append(pair)

    z_tables(z_inverse, mz[...], spread)
    gather[...] = jnp.zeros(gather.shape, F32)
    z_pass(0, cx // PLANES)
    for copy in z_faces:
        copy.wait()
    z_ends_of(gather, inverse_metric, zs2)
    z_halo(zh, z_inverse, zs2)
    z_ends = (
        send(zs2.at[1], zp.at[0], z2s.at[0], z2r.at[0], above),
        send(zs2.at[0], zp.at[1], z2s.at[1], z2r.at[1], below),
    )
    for copy in z_ends:
        copy.start()
    x_pass(0)
    for load in loads[3:6]:
        load.wait()
    ytab[...] = y_table(yi[...], my[...])

    def y_pass(first, last):
        pl.loop(first, last)(lambda q: along_y(q, v, parts, ytab, gyz, cyz))

    y_pass(0, cx // 2 // PLANES)
    for c in range(1, CHUNKS):
        x_pass(c)
    y_pass(cx // 2 // PLANES, cx // PLANES)
    for copy in z_ends:
        copy.wait()
    times(lambda q: z_correct(q, spread, z_inverse, zh, zp, zs2, gyz, cyz), 0, cx // 4, 2)
    for copy in corners:
        copy.wait()
    x_tables(x_inverse, mx[...], xc, tab)
    for pair in x_ends:
        for copy in pair:
            copy.wait()


def exchange(velocity, x_inverse, y_inverse, z_inverse, metric_x, metric_y, metric_z):
    _, cx, rows, cz = velocity.shape
    dma = pltpu.SemaphoreType.DMA

    def vmem(*shape):
        return pltpu.VMEM(shape, F32)

    def half(*shape):
        return pltpu.VMEM(shape, BF16)

    outs = (
        (3, cx, rows, cz),
        (2, 3, 2, rows, cz),
        (2, 6, rows, cz),
        (2, 6, rows, cz),
        (3 * cx + 32, 128),
        (2, 3, cx, rows, cz),
        (3, cx, rows, cz),
    )
    return pl.pallas_call(
        exchange_kernel,
        out_shape=tuple(jax.ShapeDtypeStruct(shape, F32) for shape in outs),
        in_specs=[pl.BlockSpec(memory_space=pltpu.HBM)] * 7,
        out_specs=(pl.BlockSpec(memory_space=pltpu.VMEM),) * len(outs),
        scratch_shapes=[
            vmem(cx, cx), vmem(rows, rows), vmem(cz, cz), vmem(1, cx), vmem(1, rows), vmem(1, cz),
            vmem(2, 8, 128), vmem(2, 8, 128), vmem(2 * (cx + 8), 128),
            half(6, cx, rows, 2 * cz),
            *[vmem(2, cx // 2, 8, 2 * rows)] * 4, vmem(2 * rows, cz),
            half(rows, 3 * rows), half(2 * cz, 2 * cz), half(256, 6 * cz),
            dma((7,)),
            dma((2, CHUNKS)), dma((2, CHUNKS)), dma((2, CHUNKS)), dma((2, CHUNKS)),
            dma((2,)), dma((2,)), dma((2,)), dma((2,)), dma((2,)), dma((2,)),
        ],
        compiler_params=pltpu.CompilerParams(
            collective_id=0, has_side_effects=True, vmem_limit_bytes=22 * MIB),
        name="exchange",
    )(*[
        pltpu.with_memory_space_constraint(a, pltpu.HBM)
        for a in (velocity, x_inverse, y_inverse, z_inverse, metric_x.reshape(1, cx),
                  metric_y.reshape(1, rows), metric_z.reshape(1, cz))
    ])


def x_sweep(part, v, xh, xp, xe, tab, gx, conv, cyz):
    cx = v.shape[1]

    def cell(j):
        if j < 0:
            velocity = [xh[0, i, j + 2, part] for i in range(3)]
        elif j >= cx:
            velocity = [xh[1, i, j - cx, part] for i in range(3)]
        else:
            velocity = [v[i, j, part] for i in range(3)]
        return velocity + [a * velocity[0] for a in velocity]

    window = [cell(j) for j in range(-2, 2)]
    state = None
    for j in range(cx):
        window.append(cell(j + 2))
        fresh = []
        for f in range(6):
            d = (window[3][f] - window[1][f]) + (FAR / NEAR) * (window[4][f] - window[0][f])
            for side, line in ((0, 0), (1, cx - 1)):
                if j == line:
                    k = 3 * cx + 16 * side
                    d = d - tab[k : k + 8] * xp[side, f, part] + tab[k + 8 : k + 16] * xe[side, f, part]
            value = tile_of(tab, j) * d
            if state is not None:
                value = value + tile_of(tab, cx + j) * state[f]
            fresh.append(value)
            if j < cx - 1:
                if f < 3:
                    gx[f, j, part] = value
                else:
                    conv[f - 3, j, part] = value
        state = fresh
        window.pop(0)
    for j in range(cx - 1, -1, -1):
        if j < cx - 1:
            up = tile_of(tab, 2 * cx + j)
            state = [(gx[f, j, part] if f < 3 else conv[f - 3, j, part]) + up * state[f] for f in range(6)]
        for i in range(3):
            gx[i, j, part] = state[i]
            conv[i, j, part] = state[3 + i] + cyz[i, j, part]


def x_kernel(v, xh, xp, xe, tab, gyz, cyz, grad, conv, gx_out, conv_out, yz_sem, x_sem, c_sem):
    rows = v.shape[2]
    copies = [pltpu.make_async_copy(gyz.at[k], grad.at[:, 1 + k], yz_sem.at[k]) for k in range(2)]
    for copy in copies:
        copy.start()
    step = rows // OUT_CHUNKS
    for c in range(OUT_CHUNKS):
        times(
            lambda t: x_sweep(
                pl.ds(pl.multiple_of(t * 8, 8), 8), v, xh, xp, xe, tab, gx_out, conv_out, cyz),
            c * (step // 8), (c + 1) * (step // 8), 2)
        part = pl.ds(c * step, step)
        pair = (
            pltpu.make_async_copy(gx_out.at[:, :, part], grad.at[:, 0, :, part], x_sem.at[c]),
            pltpu.make_async_copy(conv_out.at[:, :, part], conv.at[:, :, part], c_sem.at[c]),
        )
        for copy in pair:
            copy.start()
        copies += pair
    for copy in copies:
        copy.wait()


def x_solve(v, xh, xp, xe, tab, gyz, cyz):
    _, cx, rows, cz = v.shape
    dma = pltpu.SemaphoreType.DMA
    return pl.pallas_call(
        x_kernel,
        out_shape=(
            jax.ShapeDtypeStruct((3, 3, cx, rows, cz), F32),
            jax.ShapeDtypeStruct((3, cx, rows, cz), F32),
        ),
        in_specs=[pl.BlockSpec(memory_space=pltpu.VMEM)] * 7,
        out_specs=(pl.BlockSpec(memory_space=pltpu.HBM),) * 2,
        scratch_shapes=[
            pltpu.VMEM((3, cx, rows, cz), F32),
            pltpu.VMEM((3, cx, rows, cz), F32),
            dma((2,)), dma((OUT_CHUNKS,)), dma((OUT_CHUNKS,)),
        ],
        compiler_params=pltpu.CompilerParams(vmem_limit_bytes=14 * MIB),
        name="x_solve",
    )(v, xh, xp, xe, tab, gyz, cyz)


def on_device(velocity, metric_x, metric_y, metric_z, x_inverse, y_inverse, z_inverse):
    return tuple(x_solve(*exchange(
        velocity, x_inverse, y_inverse, z_inverse, metric_x, metric_y, metric_z)))


def solution(mesh):
    return jax.shard_map(
        on_device,
        mesh=mesh,
        in_specs=(
            P(None, ("gx", "gy"), None, "gz"),
            P(("gx", "gy")),
            P(),
            P("gz"),
            P(("gx", "gy"), None),
            P(),
            P("gz", None),
        ),
        out_specs=(P(None, None, ("gx", "gy"), None, "gz"), P(None, ("gx", "gy"), None, "gz")),
        check_vma=False,
    )
```

```python
import jax
import jax.numpy as jnp
from jax import lax
from jax.experimental import pallas as pl
from jax.experimental.pallas import tpu as pltpu
from jax.sharding import PartitionSpec as P

COUPLING = 1.0 / 3.0
NEAR = 7.0 / 9.0
FAR = 1.0 / 36.0
F32 = jnp.float32
BF16 = jnp.bfloat16
MESH = pl.DeviceIdType.MESH
HIGH = lax.Precision.HIGHEST
CHUNKS = 2
OUT_CHUNKS = 6
PLANES = 8
MIB = 1 << 20


def split(values):
    high = values.astype(BF16)
    return high, (values - high.astype(F32)).astype(BF16)


def iota(shape, dim):
    return lax.broadcasted_iota(jnp.int32, shape, dim)


def band(size):
    step = iota((size, size), 1) - iota((size, size), 0)
    near = jnp.where(step == 1, NEAR, jnp.where(step == -1, -NEAR, 0.0))
    far = jnp.where(step == 2, FAR, jnp.where(step == -2, -FAR, 0.0))
    return (near + far).astype(F32)


def dot(a, b, dims=((1,), (0,)), precision=None):
    return lax.dot_general(a, b, (dims, ((), ())), precision=precision, preferred_element_type=F32)


def z_tables(z_inverse, metric, spread):
    size = z_inverse.shape[0]
    columns = z_inverse.T
    lines = [columns[k : k + 1] * metric for k in (0, 1, size - 2, size - 1)]
    row = iota((32, size), 0)
    zero = jnp.zeros((64, size), BF16)
    for field in range(6):
        table = jnp.zeros((32, size), F32)
        for k, line in enumerate(lines):
            table = jnp.where(row == 8 * k + field, line, table)
        high, low = split(table)
        spread[:, field * size : (field + 1) * size] = jnp.concatenate(
            [high, high, zero, low, low, zero], axis=0)


def z_weights(z_inverse, metric, weights):
    high, low = split(dot(z_inverse, band(z_inverse.shape[0]), precision=HIGH).T * metric)
    both = jnp.concatenate([high, low], axis=1)
    weights[...] = jnp.concatenate([both, both], axis=0)


def y_table(y_inverse, metric):
    size = y_inverse.shape[0]
    own = iota((size, size), 0) == iota((size, size), 1)
    column = jnp.sum(jnp.where(own, metric, 0.0), axis=1, keepdims=True)
    high, low = split(y_inverse)
    near, rest = split(band(size))
    product = dot(jnp.concatenate([high, low, high], axis=1), jnp.concatenate([near, near, rest], axis=0))
    high, low = split(product * column)
    return jnp.concatenate([high, high, low], axis=1)


def x_end_weights(inverse, store):
    size = inverse.shape[0]
    rows = size + 8
    step = iota((rows, size), 0) - iota((rows, size), 1) - 2
    near = jnp.where(step == 1, NEAR, jnp.where(step == -1, -NEAR, 0.0))
    far = jnp.where(step == 2, FAR, jnp.where(step == -2, -FAR, 0.0))
    taps = (near + far).astype(F32)
    for end, line in ((0, 0), (1, size - 1)):
        column = jnp.sum(taps * inverse[line : line + 1], axis=1, keepdims=True)
        store[end * rows : (end + 1) * rows] = jnp.broadcast_to(column, (rows, 128))


def x_tables(inverse, metric, corners, tab):
    size = inverse.shape[0]
    row, col = iota((size, size), 0), iota((size, size), 1)

    def pick(values, shift):
        return jnp.sum(jnp.where(col == row + shift, values, 0.0), axis=1, keepdims=True)

    def shifted(values, by):
        pad = jnp.zeros((1, values.shape[1]), F32)
        if by > 0:
            return jnp.concatenate([values[1:], pad], axis=0)
        return jnp.concatenate([pad, values[:-1]], axis=0)

    line = iota((size, 1), 0)
    below = shifted(inverse, 1)
    scale = pick(metric, 0)
    pivot = jnp.where(line < size - 1, pick(below, 1), 1.0)
    up = pick(inverse, 1) / pivot
    own = pick(inverse, 0) - up * pick(below, 0)
    before = jnp.where(line > 0, shifted(own, -1), 1.0)
    down = (pick(inverse, -1) - up * pick(below, -1)) / before
    above_scale = jnp.where(line < size - 1, pick(metric, 1), 1.0)
    below_scale = jnp.where(line > 0, pick(metric, -1), 1.0)
    for k, value in enumerate((NEAR * scale * own, down * scale / below_scale, up * scale / above_scale)):
        tab[k * size : (k + 1) * size] = jnp.broadcast_to(value, (size, 128))
    for side, end in ((0, 0), (1, size - 1)):
        own_end = inverse[end : end + 1, end : end + 1]
        other = corners[side]
        gain = (COUPLING / NEAR) / (1.0 - COUPLING * COUPLING * other * own_end)
        tab[3 * size + 16 * side : 3 * size + 16 * side + 8] = gain
        tab[3 * size + 16 * side + 8 : 3 * size + 16 * side + 16] = COUPLING * other * gain


def tile_of(table, row):
    return jnp.broadcast_to(table[row : row + 1], (8, 128))


def z_faces_of(v, corner, zs1):
    size, rows = v.shape[1:3]
    lane = iota((1, 128), 1)
    for k in range(2 * rows // 128):
        total = None
        for p in range(size // 2):
            for i in range(3):
                lines = v[i, 2 * p : 2 * p + 2].reshape(2 * rows, 128)[128 * k : 128 * k + 128]
                first = 16 * p + 4 * i
                moved = pltpu.roll(lines, first + 2, 1)
                total = moved if total is None else jnp.where((lane >= first) & (lane < first + 4), moved, total)
        got = total.T
        for p in range(size // 2):
            for side, layers in ((0, (2, 3)), (1, (0, 1))):
                lines = [got[16 * p + 4 * i + n : 16 * p + 4 * i + n + 1] for n in layers for i in range(3)]
                zs1[side, p, :, 128 * k : 128 * k + 128] = jnp.concatenate(
                    lines + [jnp.broadcast_to(corner[side], (1, 128)), jnp.zeros((1, 128), F32)], axis=0)


def z_ends_of(gather, inverse_metric, zs2):
    for k in range(gather.shape[0] // 128):
        got = gather[128 * k : 128 * k + 128].T
        for p in range(zs2.shape[1]):
            for side in range(2):
                lines = [got[16 * p + 2 * f + 1 - side : 16 * p + 2 * f + 2 - side] for f in range(6)]
                zs2[side, p, :, 128 * k : 128 * k + 128] = inverse_metric[side] * jnp.concatenate(
                    lines + [jnp.zeros((2, 128), F32)], axis=0)


def z_local(q, v, parts, ztab, gyz, cyz, gather):
    rows, cz = v.shape[2:]
    lane = iota((1, cz), 1)
    planes = [PLANES * q + k for k in range(PLANES)]
    for x in planes:
        velocity = [v[i, x] for i in range(3)]
        for field in range(6):
            value = velocity[field] if field < 3 else velocity[field - 3] * velocity[2]
            parts[field, x] = jnp.concatenate(split(value), axis=1)
    ends = [gather[k * rows : (k + 1) * rows] for k in range(2)]
    for k, x in enumerate(planes):
        got = dot(parts[:, x].reshape(6 * rows, 2 * cz), ztab[...])
        got = got[:, :cz] + got[:, cz:]
        for f in range(6):
            values = got[f * rows : (f + 1) * rows]
            if f < 3:
                gyz[1, f, x] = values
            else:
                cyz[f - 3, x] = values
            first = 8 * PLANES * q + 16 * (k // 2) + 2 * f
            kept = (lane >= first) & (lane < first + 2)
            ends[k % 2] = jnp.where(kept, pltpu.roll(values, first + 1, 1), ends[k % 2])
    for k in range(2):
        gather[k * rows : (k + 1) * rows] = ends[k]


def beside(halo, near, far):
    def six(first):
        lines = halo[first : first + 3]
        pad = jnp.zeros((2, lines.shape[1]), F32)
        return jnp.concatenate([lines, lines * lines[2:3], pad], axis=0)

    return six(near), six(far)


def z_halo(zh, z_inverse, zs2):
    size = z_inverse.shape[0]
    weights = []
    for line in (0, size - 1):
        a, b, c, d = (z_inverse[line : line + 1, k : k + 1] for k in (0, 1, size - 2, size - 1))
        weights.append((-NEAR * a - FAR * b, -FAR * a, NEAR * d + FAR * c, FAR * d))
    for p in range(zh.shape[1]):
        layers = beside(zh[0, p], 3, 0) + beside(zh[1, p], 0, 3)
        for side in range(2):
            total = zs2[side, p]
            for weight, layer in zip(weights[side], layers):
                total = total + weight * layer
            zs2[side, p] = total


def z_correct(q, spread, z_inverse, zh, zp, zs2, gyz, cyz):
    rows, cz = gyz.shape[3:]
    square = COUPLING * COUPLING
    own = (z_inverse[0:1, 0:1], z_inverse[cz - 1 : cz, cz - 1 : cz])
    lines = []
    for k in range(2):
        p = 2 * q + k
        terms = []
        for side, sign in ((0, -1.0), (1, 1.0)):
            halo = zh[side, p]
            near, far = beside(halo, 3 - 3 * side, 3 * side)
            other = halo[6:7, 0:1]
            gain = COUPLING / (1.0 - square * other * own[side])
            first = (sign * NEAR) * near + (sign * FAR) * far - gain * zp[side, p]
            first = first + (COUPLING * other * gain) * zs2[side, p]
            second = (sign * FAR) * near
            terms += [first, second] if side == 0 else [second, first]
        high, low = split(jnp.concatenate(terms, axis=0))
        lines += [high.astype(F32), low.astype(F32)]
    turned = jnp.concatenate(lines, axis=0).T
    turned = jnp.concatenate([turned, pltpu.roll(turned, 64, 1)], axis=0).astype(BF16)
    more = dot(jnp.concatenate([turned, turned], axis=1), spread[...])
    planes = pl.ds(4 * q, 4)
    for i in range(3):
        gyz[1, i, planes] = gyz[1, i, planes] + more[:, i * cz : (i + 1) * cz].reshape(4, rows, cz)
        cyz[i, planes] = cyz[i, planes] + more[:, (3 + i) * cz : (4 + i) * cz].reshape(4, rows, cz)


def x_local(t, v, wtab, xe):
    part = pl.ds(pl.multiple_of(t * 8, 8), 8)
    size = v.shape[1]
    ends = [[None] * 6, [None] * 6]
    for j in range(size):
        velocity = [v[i, j, part] for i in range(3)]
        fields = velocity + [a * velocity[0] for a in velocity]
        for end in range(2):
            weight = tile_of(wtab, end * (size + 8) + j + 2)
            for f in range(6):
                term = weight * fields[f]
                ends[end][f] = term if ends[end][f] is None else ends[end][f] + term
    for end in range(2):
        for f in range(6):
            xe[end, f, part] = ends[end][f]


def x_halo(t, size, xh, wtab, xe):
    part = pl.ds(pl.multiple_of(t * 8, 8), 8)
    ends = [[xe[end, f, part] for f in range(6)] for end in range(2)]
    for side in range(2):
        for layer in range(2):
            j = layer - 2 if side == 0 else size + layer
            velocity = [xh[side, i, layer, part] for i in range(3)]
            fields = velocity + [a * velocity[0] for a in velocity]
            for end in range(2):
                weight = tile_of(wtab, end * (size + 8) + j + 2)
                for f in range(6):
                    ends[end][f] = ends[end][f] + weight * fields[f]
    for end in range(2):
        for f in range(6):
            xe[end, f, part] = ends[end][f]


def along_y(q, v, parts, ytab, gyz, cyz):
    cz = v.shape[3]
    planes = [PLANES * q + k for k in range(PLANES)]

    def apply(pieces):
        high = jnp.concatenate([a[0] for a in pieces], axis=1)
        low = jnp.concatenate([a[1] for a in pieces], axis=1)
        return dot(ytab[...], jnp.concatenate([high, low, high], axis=0))

    def held(field):
        got = [parts[field, x] for x in planes]
        return [(g[:, :cz], g[:, cz:]) for g in got]

    for i in range(3):
        got = apply(held(i))
        for k, x in enumerate(planes):
            gyz[0, i, x] = got[:, k * cz : (k + 1) * cz]
        got = apply(held(4) if i == 2 else [split(v[i, x] * v[1, x]) for x in planes])
        for k, x in enumerate(planes):
            cyz[i, x] = cyz[i, x] + got[:, k * cz : (k + 1) * cz]


def times(body, start, stop, unit):
    @pl.loop(start // unit, stop // unit)
    def _(t):
        for k in range(unit):
            body(unit * t + k)


def exchange_kernel(
    v_hbm, xi_hbm, yi_hbm, zi_hbm, mx_hbm, my_hbm, mz_hbm,
    v, xh, xp, xe, tab, gyz, cyz,
    xi, yi, zi, mx, my, mz, xcs, xc, wtab, parts, zs1, zs2, zh, zp, gather, ytab, ztab, spread,
    load_sem, x1s, x1r, x2s, x2r, z1s, z1r, z2s, z2r, xcsem, xcrecv,
):
    gx, gy, gz = lax.axis_index("gx"), lax.axis_index("gy"), lax.axis_index("gz")
    nx, ny, nz = lax.axis_size("gx"), lax.axis_size("gy"), lax.axis_size("gz")
    me = gx * ny + gy
    count = nx * ny
    xl, xr = lax.rem(me + count - 1, count), lax.rem(me + 1, count)
    left = {"gx": xl // ny, "gy": lax.rem(xl, ny)}
    right = {"gx": xr // ny, "gy": lax.rem(xr, ny)}
    below = {"gz": lax.rem(gz + nz - 1, nz)}
    above = {"gz": lax.rem(gz + 1, nz)}
    barrier = pltpu.get_barrier_semaphore()
    for device in (left, right, below, above):
        pl.semaphore_signal(barrier, inc=1, device_id=device, device_id_type=MESH)

    loads = [
        pltpu.make_async_copy(src, dst, load_sem.at[k])
        for k, (src, dst) in enumerate(
            ((zi_hbm, zi), (xi_hbm, xi), (v_hbm, v), (yi_hbm, yi), (mx_hbm, mx), (my_hbm, my), (mz_hbm, mz)))
    ]
    for load in loads:
        load.start()
    cx, rows, cz = v.shape[1:]

    def send(src, dst, s, r, device):
        return pltpu.make_async_remote_copy(
            src_ref=src, dst_ref=dst, send_sem=s, recv_sem=r, device_id=device, device_id_type=MESH)

    step = rows // CHUNKS
    pl.semaphore_wait(barrier, 4)
    faces = []
    for c in range(CHUNKS):
        part = pl.ds(c * step, step)
        pair = (
            send(v_hbm.at[:, pl.ds(cx - 2, 2), part], xh.at[0, :, :, part], x1s.at[0, c], x1r.at[0, c], right),
            send(v_hbm.at[:, pl.ds(0, 2), part], xh.at[1, :, :, part], x1s.at[1, c], x1r.at[1, c], left),
        )
        for copy in pair:
            copy.start()
        faces.append(pair)
    loads[0].wait()
    loads[1].wait()
    loads[6].wait()
    z_inverse = zi[...]
    corner = (z_inverse[0:1, 0:1], z_inverse[cz - 1 : cz, cz - 1 : cz])
    z_weights(z_inverse, mz[...], ztab)
    x_inverse = xi[...]
    xcs[0] = jnp.broadcast_to(x_inverse[0:1, 0:1], (8, 128))
    xcs[1] = jnp.broadcast_to(x_inverse[cx - 1 : cx, cx - 1 : cx], (8, 128))
    x_end_weights(x_inverse, wtab)
    loads[2].wait()
    z_faces_of(v, corner, zs1)
    corners = (
        send(xcs.at[1], xc.at[0], xcsem.at[0], xcrecv.at[0], right),
        send(xcs.at[0], xc.at[1], xcsem.at[1], xcrecv.at[1], left),
    )
    for copy in corners:
        copy.start()
    z_faces = (
        send(zs1.at[1], zh.at[0], z1s.at[0], z1r.at[0], above),
        send(zs1.at[0], zh.at[1], z1s.at[1], z1r.at[1], below),
    )
    for copy in z_faces:
        copy.start()
    times(lambda t: x_local(t, v, wtab, xe), 0, rows // 8, 2)

    inverse_metric = (1.0 / mz[:, 0:1], 1.0 / mz[:, cz - 1 : cz])

    def z_pass(first, last):
        pl.loop(first, last)(lambda p: z_local(p, v, parts, ztab, gyz, cyz, gather))

    x_ends = []

    def x_pass(c):
        for copy in faces[c]:
            copy.wait()
        times(lambda t: x_halo(t, cx, xh, wtab, xe), c * (step // 8), (c + 1) * (step // 8), 2)
        part = pl.ds(c * step, step)
        pair = (
            send(xe.at[1, :, part], xp.at[0, :, part], x2s.at[0, c], x2r.at[0, c], right),
            send(xe.at[0, :, part], xp.at[1, :, part], x2s.at[1, c], x2r.at[1, c], left),
        )
        for copy in pair:
            copy.start()
        x_ends.append(pair)

    z_tables(z_inverse, mz[...], spread)
    gather[...] = jnp.zeros(gather.shape, F32)
    z_pass(0, cx // 2 // PLANES)
    x_pass(0)
    z_pass(cx // 2 // PLANES, cx // PLANES)
    for copy in z_faces:
        copy.wait()
    z_ends_of(gather, inverse_metric, zs2)
    z_halo(zh, z_inverse, zs2)
    z_ends = (
        send(zs2.at[1], zp.at[0], z2s.at[0], z2r.at[0], above),
        send(zs2.at[0], zp.at[1], z2s.at[1], z2r.at[1], below),
    )
    for copy in z_ends:
        copy.start()
    for c in range(1, CHUNKS):
        x_pass(c)
    for load in loads[3:6]:
        load.wait()
    ytab[...] = y_table(yi[...], my[...])

    def y_pass(first, last):
        pl.loop(first, last)(lambda q: along_y(q, v, parts, ytab, gyz, cyz))

    y_pass(0, cx // PLANES)
    for copy in z_ends:
        copy.wait()
    times(lambda q: z_correct(q, spread, z_inverse, zh, zp, zs2, gyz, cyz), 0, cx // 4, 2)
    for copy in corners:
        copy.wait()
    x_tables(x_inverse, mx[...], xc, tab)
    for pair in x_ends:
        for copy in pair:
            copy.wait()


def exchange(velocity, x_inverse, y_inverse, z_inverse, metric_x, metric_y, metric_z):
    _, cx, rows, cz = velocity.shape
    dma = pltpu.SemaphoreType.DMA

    def vmem(*shape):
        return pltpu.VMEM(shape, F32)

    def half(*shape):
        return pltpu.VMEM(shape, BF16)

    outs = (
        (3, cx, rows, cz),
        (2, 3, 2, rows, cz),
        (2, 6, rows, cz),
        (2, 6, rows, cz),
        (3 * cx + 32, 128),
        (2, 3, cx, rows, cz),
        (3, cx, rows, cz),
    )
    return pl.pallas_call(
        exchange_kernel,
        out_shape=tuple(jax.ShapeDtypeStruct(shape, F32) for shape in outs),
        in_specs=[pl.BlockSpec(memory_space=pltpu.HBM)] * 7,
        out_specs=(pl.BlockSpec(memory_space=pltpu.VMEM),) * len(outs),
        scratch_shapes=[
            vmem(cx, cx), vmem(rows, rows), vmem(cz, cz), vmem(1, cx), vmem(1, rows), vmem(1, cz),
            vmem(2, 8, 128), vmem(2, 8, 128), vmem(2 * (cx + 8), 128),
            half(6, cx, rows, 2 * cz),
            *[vmem(2, cx // 2, 8, 2 * rows)] * 4, vmem(2 * rows, cz),
            half(rows, 3 * rows), half(2 * cz, 2 * cz), half(256, 6 * cz),
            dma((7,)),
            dma((2, CHUNKS)), dma((2, CHUNKS)), dma((2, CHUNKS)), dma((2, CHUNKS)),
            dma((2,)), dma((2,)), dma((2,)), dma((2,)), dma((2,)), dma((2,)),
        ],
        compiler_params=pltpu.CompilerParams(
            collective_id=0, has_side_effects=True, vmem_limit_bytes=22 * MIB),
        name="exchange",
    )(*[
        pltpu.with_memory_space_constraint(a, pltpu.HBM)
        for a in (velocity, x_inverse, y_inverse, z_inverse, metric_x.reshape(1, cx),
                  metric_y.reshape(1, rows), metric_z.reshape(1, cz))
    ])


def x_sweep(part, v, xh, xp, xe, tab, gx, conv, cyz):
    cx = v.shape[1]

    def cell(j):
        if j < 0:
            velocity = [xh[0, i, j + 2, part] for i in range(3)]
        elif j >= cx:
            velocity = [xh[1, i, j - cx, part] for i in range(3)]
        else:
            velocity = [v[i, j, part] for i in range(3)]
        return velocity + [a * velocity[0] for a in velocity]

    window = [cell(j) for j in range(-2, 2)]
    state = None
    for j in range(cx):
        window.append(cell(j + 2))
        fresh = []
        for f in range(6):
            d = (window[3][f] - window[1][f]) + (FAR / NEAR) * (window[4][f] - window[0][f])
            for side, line in ((0, 0), (1, cx - 1)):
                if j == line:
                    k = 3 * cx + 16 * side
                    d = d - tab[k : k + 8] * xp[side, f, part] + tab[k + 8 : k + 16] * xe[side, f, part]
            value = tile_of(tab, j) * d
            if state is not None:
                value = value + tile_of(tab, cx + j) * state[f]
            fresh.append(value)
            if j < cx - 1:
                if f < 3:
                    gx[f, j, part] = value
                else:
                    conv[f - 3, j, part] = value
        state = fresh
        window.pop(0)
    for j in range(cx - 1, -1, -1):
        if j < cx - 1:
            up = tile_of(tab, 2 * cx + j)
            state = [(gx[f, j, part] if f < 3 else conv[f - 3, j, part]) + up * state[f] for f in range(6)]
        for i in range(3):
            gx[i, j, part] = state[i]
            conv[i, j, part] = state[3 + i] + cyz[i, j, part]


def x_kernel(v, xh, xp, xe, tab, gyz, cyz, grad, conv, gx_out, conv_out, yz_sem, x_sem, c_sem):
    rows = v.shape[2]
    copies = [pltpu.make_async_copy(gyz.at[k], grad.at[:, 1 + k], yz_sem.at[k]) for k in range(2)]
    for copy in copies:
        copy.start()
    step = rows // OUT_CHUNKS
    for c in range(OUT_CHUNKS):
        times(
            lambda t: x_sweep(
                pl.ds(pl.multiple_of(t * 8, 8), 8), v, xh, xp, xe, tab, gx_out, conv_out, cyz),
            c * (step // 8), (c + 1) * (step // 8), 2)
        part = pl.ds(c * step, step)
        pair = (
            pltpu.make_async_copy(gx_out.at[:, :, part], grad.at[:, 0, :, part], x_sem.at[c]),
            pltpu.make_async_copy(conv_out.at[:, :, part], conv.at[:, :, part], c_sem.at[c]),
        )
        for copy in pair:
            copy.start()
        copies += pair
    for copy in copies:
        copy.wait()


def x_solve(v, xh, xp, xe, tab, gyz, cyz):
    _, cx, rows, cz = v.shape
    dma = pltpu.SemaphoreType.DMA
    return pl.pallas_call(
        x_kernel,
        out_shape=(
            jax.ShapeDtypeStruct((3, 3, cx, rows, cz), F32),
            jax.ShapeDtypeStruct((3, cx, rows, cz), F32),
        ),
        in_specs=[pl.BlockSpec(memory_space=pltpu.VMEM)] * 7,
        out_specs=(pl.BlockSpec(memory_space=pltpu.HBM),) * 2,
        scratch_shapes=[
            pltpu.VMEM((3, cx, rows, cz), F32),
            pltpu.VMEM((3, cx, rows, cz), F32),
            dma((2,)), dma((OUT_CHUNKS,)), dma((OUT_CHUNKS,)),
        ],
        compiler_params=pltpu.CompilerParams(vmem_limit_bytes=14 * MIB),
        name="x_solve",
    )(v, xh, xp, xe, tab, gyz, cyz)


def on_device(velocity, metric_x, metric_y, metric_z, x_inverse, y_inverse, z_inverse):
    return tuple(x_solve(*exchange(
        velocity, x_inverse, y_inverse, z_inverse, metric_x, metric_y, metric_z)))


def solution(mesh):
    return jax.shard_map(
        on_device,
        mesh=mesh,
        in_specs=(
            P(None, ("gx", "gy"), None, "gz"),
            P(("gx", "gy")),
            P(),
            P("gz"),
            P(("gx", "gy"), None),
            P(),
            P("gz", None),
        ),
        out_specs=(P(None, None, ("gx", "gy"), None, "gz"), P(None, ("gx", "gy"), None, "gz")),
        check_vma=False,
    )
```

```python
import jax
import jax.numpy as jnp
from jax import lax
from jax.experimental import pallas as pl
from jax.experimental.pallas import tpu as pltpu
from jax.sharding import PartitionSpec as P

COUPLING = 1.0 / 3.0
NEAR = 7.0 / 9.0
FAR = 1.0 / 36.0
F32 = jnp.float32
BF16 = jnp.bfloat16
MESH = pl.DeviceIdType.MESH
HIGH = lax.Precision.HIGHEST
CHUNKS = 2
OUT_CHUNKS = 6
PLANES = 8
MIB = 1 << 20


def split(values):
    high = values.astype(BF16)
    return high, (values - high.astype(F32)).astype(BF16)


def iota(shape, dim):
    return lax.broadcasted_iota(jnp.int32, shape, dim)


def band(size):
    step = iota((size, size), 1) - iota((size, size), 0)
    near = jnp.where(step == 1, NEAR, jnp.where(step == -1, -NEAR, 0.0))
    far = jnp.where(step == 2, FAR, jnp.where(step == -2, -FAR, 0.0))
    return (near + far).astype(F32)


def dot(a, b, dims=((1,), (0,)), precision=None):
    return lax.dot_general(a, b, (dims, ((), ())), precision=precision, preferred_element_type=F32)


def z_tables(z_inverse, metric, spread):
    size = z_inverse.shape[0]
    columns = z_inverse.T
    lines = [columns[k : k + 1] * metric for k in (0, 1, size - 2, size - 1)]
    row = iota((32, size), 0)
    zero = jnp.zeros((64, size), BF16)
    for field in range(6):
        table = jnp.zeros((32, size), F32)
        for k, line in enumerate(lines):
            table = jnp.where(row == 8 * k + field, line, table)
        high, low = split(table)
        spread[:, field * size : (field + 1) * size] = jnp.concatenate(
            [high, high, zero, low, low, zero], axis=0)


def z_weights(z_inverse, metric, weights):
    high, low = split(dot(z_inverse, band(z_inverse.shape[0]), precision=HIGH).T * metric)
    both = jnp.concatenate([high, low], axis=1)
    weights[...] = jnp.concatenate([both, both], axis=0)


def y_table(y_inverse, metric):
    size = y_inverse.shape[0]
    own = iota((size, size), 0) == iota((size, size), 1)
    column = jnp.sum(jnp.where(own, metric, 0.0), axis=1, keepdims=True)
    high, low = split(y_inverse)
    near, rest = split(band(size))
    product = dot(jnp.concatenate([high, low, high], axis=1), jnp.concatenate([near, near, rest], axis=0))
    high, low = split(product * column)
    return jnp.concatenate([high, high, low], axis=1)


def x_end_weights(inverse, store):
    size = inverse.shape[0]
    rows = size + 8
    step = iota((rows, size), 0) - iota((rows, size), 1) - 2
    near = jnp.where(step == 1, NEAR, jnp.where(step == -1, -NEAR, 0.0))
    far = jnp.where(step == 2, FAR, jnp.where(step == -2, -FAR, 0.0))
    taps = (near + far).astype(F32)
    for end, line in ((0, 0), (1, size - 1)):
        column = jnp.sum(taps * inverse[line : line + 1], axis=1, keepdims=True)
        store[end * rows : (end + 1) * rows] = jnp.broadcast_to(column, (rows, 128))


def x_tables(inverse, metric, corners, tab):
    size = inverse.shape[0]
    row, col = iota((size, size), 0), iota((size, size), 1)

    def pick(values, shift):
        return jnp.sum(jnp.where(col == row + shift, values, 0.0), axis=1, keepdims=True)

    def shifted(values, by):
        pad = jnp.zeros((1, values.shape[1]), F32)
        if by > 0:
            return jnp.concatenate([values[1:], pad], axis=0)
        return jnp.concatenate([pad, values[:-1]], axis=0)

    line = iota((size, 1), 0)
    below = shifted(inverse, 1)
    scale = pick(metric, 0)
    pivot = jnp.where(line < size - 1, pick(below, 1), 1.0)
    up = pick(inverse, 1) / pivot
    own = pick(inverse, 0) - up * pick(below, 0)
    before = jnp.where(line > 0, shifted(own, -1), 1.0)
    down = (pick(inverse, -1) - up * pick(below, -1)) / before
    above_scale = jnp.where(line < size - 1, pick(metric, 1), 1.0)
    below_scale = jnp.where(line > 0, pick(metric, -1), 1.0)
    for k, value in enumerate((NEAR * scale * own, down * scale / below_scale, up * scale / above_scale)):
        tab[k * size : (k + 1) * size] = jnp.broadcast_to(value, (size, 128))
    for side, end in ((0, 0), (1, size - 1)):
        own_end = inverse[end : end + 1, end : end + 1]
        other = corners[side]
        gain = (COUPLING / NEAR) / (1.0 - COUPLING * COUPLING * other * own_end)
        tab[3 * size + 16 * side : 3 * size + 16 * side + 8] = gain
        tab[3 * size + 16 * side + 8 : 3 * size + 16 * side + 16] = COUPLING * other * gain


def tile_of(table, row):
    return jnp.broadcast_to(table[row : row + 1], (8, 128))


def z_faces_of(v, corner, zs1):
    size, rows = v.shape[1:3]
    lane = iota((1, 128), 1)
    for k in range(2 * rows // 128):
        total = None
        for p in range(size // 2):
            for i in range(3):
                lines = v[i, 2 * p : 2 * p + 2].reshape(2 * rows, 128)[128 * k : 128 * k + 128]
                first = 16 * p + 4 * i
                moved = pltpu.roll(lines, first + 2, 1)
                total = moved if total is None else jnp.where((lane >= first) & (lane < first + 4), moved, total)
        got = total.T
        for p in range(size // 2):
            for side, layers in ((0, (2, 3)), (1, (0, 1))):
                lines = [got[16 * p + 4 * i + n : 16 * p + 4 * i + n + 1] for n in layers for i in range(3)]
                zs1[side, p, :, 128 * k : 128 * k + 128] = jnp.concatenate(
                    lines + [jnp.broadcast_to(corner[side], (1, 128)), jnp.zeros((1, 128), F32)], axis=0)


def z_ends_of(gather, inverse_metric, zs2):
    for k in range(gather.shape[0] // 128):
        got = gather[128 * k : 128 * k + 128].T
        for p in range(zs2.shape[1]):
            for side in range(2):
                lines = [got[16 * p + 2 * f + 1 - side : 16 * p + 2 * f + 2 - side] for f in range(6)]
                zs2[side, p, :, 128 * k : 128 * k + 128] = inverse_metric[side] * jnp.concatenate(
                    lines + [jnp.zeros((2, 128), F32)], axis=0)


def z_local(q, v, parts, ztab, gyz, cyz, gather):
    rows, cz = v.shape[2:]
    lane = iota((1, cz), 1)
    planes = [PLANES * q + k for k in range(PLANES)]
    for x in planes:
        velocity = [v[i, x] for i in range(3)]
        for field in range(6):
            value = velocity[field] if field < 3 else velocity[field - 3] * velocity[2]
            parts[field, x] = jnp.concatenate(split(value), axis=1)
    ends = [gather[k * rows : (k + 1) * rows] for k in range(2)]
    for k, x in enumerate(planes):
        got = dot(parts[:, x].reshape(6 * rows, 2 * cz), ztab[...])
        got = got[:, :cz] + got[:, cz:]
        for f in range(6):
            values = got[f * rows : (f + 1) * rows]
            if f < 3:
                gyz[1, f, x] = values
            else:
                cyz[f - 3, x] = values
            first = 8 * PLANES * q + 16 * (k // 2) + 2 * f
            kept = (lane >= first) & (lane < first + 2)
            ends[k % 2] = jnp.where(kept, pltpu.roll(values, first + 1, 1), ends[k % 2])
    for k in range(2):
        gather[k * rows : (k + 1) * rows] = ends[k]


def beside(halo, near, far):
    def six(first):
        lines = halo[first : first + 3]
        pad = jnp.zeros((2, lines.shape[1]), F32)
        return jnp.concatenate([lines, lines * lines[2:3], pad], axis=0)

    return six(near), six(far)


def z_halo(zh, z_inverse, zs2):
    size = z_inverse.shape[0]
    weights = []
    for line in (0, size - 1):
        a, b, c, d = (z_inverse[line : line + 1, k : k + 1] for k in (0, 1, size - 2, size - 1))
        weights.append((-NEAR * a - FAR * b, -FAR * a, NEAR * d + FAR * c, FAR * d))
    for p in range(zh.shape[1]):
        layers = beside(zh[0, p], 3, 0) + beside(zh[1, p], 0, 3)
        for side in range(2):
            total = zs2[side, p]
            for weight, layer in zip(weights[side], layers):
                total = total + weight * layer
            zs2[side, p] = total


def z_correct(q, spread, z_inverse, zh, zp, zs2, gyz, cyz, gz_out, cyz_out):
    rows, cz = gyz.shape[3:]
    square = COUPLING * COUPLING
    own = (z_inverse[0:1, 0:1], z_inverse[cz - 1 : cz, cz - 1 : cz])
    lines = []
    for k in range(2):
        p = 2 * q + k
        terms = []
        for side, sign in ((0, -1.0), (1, 1.0)):
            halo = zh[side, p]
            near, far = beside(halo, 3 - 3 * side, 3 * side)
            other = halo[6:7, 0:1]
            gain = COUPLING / (1.0 - square * other * own[side])
            first = (sign * NEAR) * near + (sign * FAR) * far - gain * zp[side, p]
            first = first + (COUPLING * other * gain) * zs2[side, p]
            second = (sign * FAR) * near
            terms += [first, second] if side == 0 else [second, first]
        high, low = split(jnp.concatenate(terms, axis=0))
        lines += [high.astype(F32), low.astype(F32)]
    turned = jnp.concatenate(lines, axis=0).T
    turned = jnp.concatenate([turned, pltpu.roll(turned, 64, 1)], axis=0).astype(BF16)
    more = dot(jnp.concatenate([turned, turned], axis=1), spread[...])
    planes = pl.ds(4 * q, 4)
    for i in range(3):
        gz_out[i, planes] = gyz[1, i, planes] + more[:, i * cz : (i + 1) * cz].reshape(4, rows, cz)
        cyz_out[i, planes] = cyz[i, planes] + more[:, (3 + i) * cz : (4 + i) * cz].reshape(4, rows, cz)


def x_local(t, v, wtab, xe):
    part = pl.ds(pl.multiple_of(t * 8, 8), 8)
    size = v.shape[1]
    ends = [[None] * 6, [None] * 6]
    for j in range(size):
        velocity = [v[i, j, part] for i in range(3)]
        fields = velocity + [a * velocity[0] for a in velocity]
        for end in range(2):
            weight = tile_of(wtab, end * (size + 8) + j + 2)
            for f in range(6):
                term = weight * fields[f]
                ends[end][f] = term if ends[end][f] is None else ends[end][f] + term
    for end in range(2):
        for f in range(6):
            xe[end, f, part] = ends[end][f]


def x_halo(t, size, xh, wtab, xe):
    part = pl.ds(pl.multiple_of(t * 8, 8), 8)
    ends = [[xe[end, f, part] for f in range(6)] for end in range(2)]
    for side in range(2):
        for layer in range(2):
            j = layer - 2 if side == 0 else size + layer
            velocity = [xh[side, i, layer, part] for i in range(3)]
            fields = velocity + [a * velocity[0] for a in velocity]
            for end in range(2):
                weight = tile_of(wtab, end * (size + 8) + j + 2)
                for f in range(6):
                    ends[end][f] = ends[end][f] + weight * fields[f]
    for end in range(2):
        for f in range(6):
            xe[end, f, part] = ends[end][f]


def along_y(q, v, parts, ytab, gyz, cyz):
    cz = v.shape[3]
    planes = [PLANES * q + k for k in range(PLANES)]

    def apply(pieces):
        high = jnp.concatenate([a[0] for a in pieces], axis=1)
        low = jnp.concatenate([a[1] for a in pieces], axis=1)
        return dot(ytab[...], jnp.concatenate([high, low, high], axis=0))

    def held(field):
        got = [parts[field, x] for x in planes]
        return [(g[:, :cz], g[:, cz:]) for g in got]

    for i in range(3):
        got = apply(held(i))
        for k, x in enumerate(planes):
            gyz[0, i, x] = got[:, k * cz : (k + 1) * cz]
        got = apply(held(4) if i == 2 else [split(v[i, x] * v[1, x]) for x in planes])
        for k, x in enumerate(planes):
            cyz[i, x] = cyz[i, x] + got[:, k * cz : (k + 1) * cz]


def times(body, start, stop, unit):
    @pl.loop(start // unit, stop // unit)
    def _(t):
        for k in range(unit):
            body(unit * t + k)


def exchange_kernel(
    v_hbm, xi_hbm, yi_hbm, zi_hbm, mx_hbm, my_hbm, mz_hbm,
    v, xh, xp, xe, tab, gyz, cyz, zi, zh, zp, zs2, spread,
    xi, yi, mx, my, mz, xcs, xc, wtab, parts, zs1, gather, ytab, ztab,
    load_sem, x1s, x1r, x2s, x2r, z1s, z1r, z2s, z2r, xcsem, xcrecv,
):
    gx, gy, gz = lax.axis_index("gx"), lax.axis_index("gy"), lax.axis_index("gz")
    nx, ny, nz = lax.axis_size("gx"), lax.axis_size("gy"), lax.axis_size("gz")
    me = gx * ny + gy
    count = nx * ny
    xl, xr = lax.rem(me + count - 1, count), lax.rem(me + 1, count)
    left = {"gx": xl // ny, "gy": lax.rem(xl, ny)}
    right = {"gx": xr // ny, "gy": lax.rem(xr, ny)}
    below = {"gz": lax.rem(gz + nz - 1, nz)}
    above = {"gz": lax.rem(gz + 1, nz)}
    barrier = pltpu.get_barrier_semaphore()
    for device in (left, right, below, above):
        pl.semaphore_signal(barrier, inc=1, device_id=device, device_id_type=MESH)

    loads = [
        pltpu.make_async_copy(src, dst, load_sem.at[k])
        for k, (src, dst) in enumerate(
            ((zi_hbm, zi), (xi_hbm, xi), (v_hbm, v), (yi_hbm, yi), (mx_hbm, mx), (my_hbm, my), (mz_hbm, mz)))
    ]
    for load in loads:
        load.start()
    cx, rows, cz = v.shape[1:]

    def send(src, dst, s, r, device):
        return pltpu.make_async_remote_copy(
            src_ref=src, dst_ref=dst, send_sem=s, recv_sem=r, device_id=device, device_id_type=MESH)

    step = rows // CHUNKS
    pl.semaphore_wait(barrier, 4)
    faces = []
    for c in range(CHUNKS):
        part = pl.ds(c * step, step)
        pair = (
            send(v_hbm.at[:, pl.ds(cx - 2, 2), part], xh.at[0, :, :, part], x1s.at[0, c], x1r.at[0, c], right),
            send(v_hbm.at[:, pl.ds(0, 2), part], xh.at[1, :, :, part], x1s.at[1, c], x1r.at[1, c], left),
        )
        for copy in pair:
            copy.start()
        faces.append(pair)
    loads[0].wait()
    loads[1].wait()
    loads[6].wait()
    z_inverse = zi[...]
    corner = (z_inverse[0:1, 0:1], z_inverse[cz - 1 : cz, cz - 1 : cz])
    z_weights(z_inverse, mz[...], ztab)
    x_inverse = xi[...]
    xcs[0] = jnp.broadcast_to(x_inverse[0:1, 0:1], (8, 128))
    xcs[1] = jnp.broadcast_to(x_inverse[cx - 1 : cx, cx - 1 : cx], (8, 128))
    x_end_weights(x_inverse, wtab)
    loads[2].wait()
    z_faces_of(v, corner, zs1)
    corners = (
        send(xcs.at[1], xc.at[0], xcsem.at[0], xcrecv.at[0], right),
        send(xcs.at[0], xc.at[1], xcsem.at[1], xcrecv.at[1], left),
    )
    for copy in corners:
        copy.start()
    z_faces = (
        send(zs1.at[1], zh.at[0], z1s.at[0], z1r.at[0], above),
        send(zs1.at[0], zh.at[1], z1s.at[1], z1r.at[1], below),
    )
    for copy in z_faces:
        copy.start()
    times(lambda t: x_local(t, v, wtab, xe), 0, rows // 8, 2)

    inverse_metric = (1.0 / mz[:, 0:1], 1.0 / mz[:, cz - 1 : cz])

    def z_pass(first, last):
        pl.loop(first, last)(lambda p: z_local(p, v, parts, ztab, gyz, cyz, gather))

    x_ends = []

    def x_pass(c):
        for copy in faces[c]:
            copy.wait()
        times(lambda t: x_halo(t, cx, xh, wtab, xe), c * (step // 8), (c + 1) * (step // 8), 2)
        part = pl.ds(c * step, step)
        pair = (
            send(xe.at[1, :, part], xp.at[0, :, part], x2s.at[0, c], x2r.at[0, c], right),
            send(xe.at[0, :, part], xp.at[1, :, part], x2s.at[1, c], x2r.at[1, c], left),
        )
        for copy in pair:
            copy.start()
        x_ends.append(pair)

    z_tables(z_inverse, mz[...], spread)
    gather[...] = jnp.zeros(gather.shape, F32)
    z_pass(0, cx // 2 // PLANES)
    x_pass(0)
    z_pass(cx // 2 // PLANES, cx // PLANES)
    for copy in z_faces:
        copy.wait()
    z_ends_of(gather, inverse_metric, zs2)
    z_halo(zh, z_inverse, zs2)
    z_ends = (
        send(zs2.at[1], zp.at[0], z2s.at[0], z2r.at[0], above),
        send(zs2.at[0], zp.at[1], z2s.at[1], z2r.at[1], below),
    )
    for copy in z_ends:
        copy.start()
    for c in range(1, CHUNKS):
        x_pass(c)
    for load in loads[3:6]:
        load.wait()
    ytab[...] = y_table(yi[...], my[...])

    def y_pass(first, last):
        pl.loop(first, last)(lambda q: along_y(q, v, parts, ytab, gyz, cyz))

    y_pass(0, cx // PLANES)
    for copy in z_ends:
        copy.wait()
    for copy in corners:
        copy.wait()
    x_tables(x_inverse, mx[...], xc, tab)
    for pair in x_ends:
        for copy in pair:
            copy.wait()


def exchange(velocity, x_inverse, y_inverse, z_inverse, metric_x, metric_y, metric_z):
    _, cx, rows, cz = velocity.shape
    dma = pltpu.SemaphoreType.DMA

    def vmem(*shape):
        return pltpu.VMEM(shape, F32)

    def half(*shape):
        return pltpu.VMEM(shape, BF16)

    outs = (
        (3, cx, rows, cz),
        (2, 3, 2, rows, cz),
        (2, 6, rows, cz),
        (2, 6, rows, cz),
        (3 * cx + 32, 128),
        (2, 3, cx, rows, cz),
        (3, cx, rows, cz),
        (cz, cz),
        *[(2, cx // 2, 8, 2 * rows)] * 3,
    )
    return pl.pallas_call(
        exchange_kernel,
        out_shape=tuple(jax.ShapeDtypeStruct(shape, F32) for shape in outs)
        + (jax.ShapeDtypeStruct((256, 6 * cz), BF16),),
        in_specs=[pl.BlockSpec(memory_space=pltpu.HBM)] * 7,
        out_specs=(pl.BlockSpec(memory_space=pltpu.VMEM),) * (len(outs) + 1),
        scratch_shapes=[
            vmem(cx, cx), vmem(rows, rows), vmem(1, cx), vmem(1, rows), vmem(1, cz),
            vmem(2, 8, 128), vmem(2, 8, 128), vmem(2 * (cx + 8), 128),
            half(6, cx, rows, 2 * cz),
            vmem(2, cx // 2, 8, 2 * rows), vmem(2 * rows, cz),
            half(rows, 3 * rows), half(2 * cz, 2 * cz),
            dma((7,)),
            dma((2, CHUNKS)), dma((2, CHUNKS)), dma((2, CHUNKS)), dma((2, CHUNKS)),
            dma((2,)), dma((2,)), dma((2,)), dma((2,)), dma((2,)), dma((2,)),
        ],
        compiler_params=pltpu.CompilerParams(
            collective_id=0, has_side_effects=True, vmem_limit_bytes=22 * MIB),
        name="exchange",
    )(*[
        pltpu.with_memory_space_constraint(a, pltpu.HBM)
        for a in (velocity, x_inverse, y_inverse, z_inverse, metric_x.reshape(1, cx),
                  metric_y.reshape(1, rows), metric_z.reshape(1, cz))
    ])


def x_sweep(part, v, xh, xp, xe, tab, gx, conv, cyz):
    cx = v.shape[1]

    def cell(j):
        if j < 0:
            velocity = [xh[0, i, j + 2, part] for i in range(3)]
        elif j >= cx:
            velocity = [xh[1, i, j - cx, part] for i in range(3)]
        else:
            velocity = [v[i, j, part] for i in range(3)]
        return velocity + [a * velocity[0] for a in velocity]

    window = [cell(j) for j in range(-2, 2)]
    state = None
    for j in range(cx):
        window.append(cell(j + 2))
        fresh = []
        for f in range(6):
            d = (window[3][f] - window[1][f]) + (FAR / NEAR) * (window[4][f] - window[0][f])
            for side, line in ((0, 0), (1, cx - 1)):
                if j == line:
                    k = 3 * cx + 16 * side
                    d = d - tab[k : k + 8] * xp[side, f, part] + tab[k + 8 : k + 16] * xe[side, f, part]
            value = tile_of(tab, j) * d
            if state is not None:
                value = value + tile_of(tab, cx + j) * state[f]
            fresh.append(value)
            if j < cx - 1:
                if f < 3:
                    gx[f, j, part] = value
                else:
                    conv[f - 3, j, part] = value
        state = fresh
        window.pop(0)
    for j in range(cx - 1, -1, -1):
        if j < cx - 1:
            up = tile_of(tab, 2 * cx + j)
            state = [(gx[f, j, part] if f < 3 else conv[f - 3, j, part]) + up * state[f] for f in range(6)]
        for i in range(3):
            gx[i, j, part] = state[i]
            conv[i, j, part] = state[3 + i] + cyz[i, j, part]


def x_kernel(
    v, xh, xp, xe, tab, gyz, cyz, zi, zh, zp, zs2, spread, grad, conv,
    gx_out, conv_out, gz_out, cyz_out, yz_sem, x_sem, c_sem,
):
    rows = v.shape[2]
    copies = [
        pltpu.make_async_copy(gyz.at[0], grad.at[:, 1], yz_sem.at[0]),
        pltpu.make_async_copy(gz_out, grad.at[:, 2], yz_sem.at[1]),
    ]
    copies[0].start()
    z_inverse = zi[...]
    times(
        lambda q: z_correct(q, spread, z_inverse, zh, zp, zs2, gyz, cyz, gz_out, cyz_out),
        0, v.shape[1] // 4, 2)
    copies[1].start()
    step = rows // OUT_CHUNKS
    for c in range(OUT_CHUNKS):
        times(
            lambda t: x_sweep(
                pl.ds(pl.multiple_of(t * 8, 8), 8), v, xh, xp, xe, tab, gx_out, conv_out, cyz_out),
            c * (step // 8), (c + 1) * (step // 8), 2)
        part = pl.ds(c * step, step)
        pair = (
            pltpu.make_async_copy(gx_out.at[:, :, part], grad.at[:, 0, :, part], x_sem.at[c]),
            pltpu.make_async_copy(conv_out.at[:, :, part], conv.at[:, :, part], c_sem.at[c]),
        )
        for copy in pair:
            copy.start()
        copies += pair
    for copy in copies:
        copy.wait()


def x_solve(*arrays):
    _, cx, rows, cz = arrays[0].shape
    dma = pltpu.SemaphoreType.DMA
    return pl.pallas_call(
        x_kernel,
        out_shape=(
            jax.ShapeDtypeStruct((3, 3, cx, rows, cz), F32),
            jax.ShapeDtypeStruct((3, cx, rows, cz), F32),
        ),
        in_specs=[pl.BlockSpec(memory_space=pltpu.VMEM)] * len(arrays),
        out_specs=(pl.BlockSpec(memory_space=pltpu.HBM),) * 2,
        scratch_shapes=[
            *[pltpu.VMEM((3, cx, rows, cz), F32)] * 4,
            dma((2,)), dma((OUT_CHUNKS,)), dma((OUT_CHUNKS,)),
        ],
        compiler_params=pltpu.CompilerParams(vmem_limit_bytes=24 * MIB),
        name="x_solve",
    )(*arrays)


def on_device(velocity, metric_x, metric_y, metric_z, x_inverse, y_inverse, z_inverse):
    return tuple(x_solve(*exchange(
        velocity, x_inverse, y_inverse, z_inverse, metric_x, metric_y, metric_z)))


def solution(mesh):
    return jax.shard_map(
        on_device,
        mesh=mesh,
        in_specs=(
            P(None, ("gx", "gy"), None, "gz"),
            P(("gx", "gy")),
            P(),
            P("gz"),
            P(("gx", "gy"), None),
            P(),
            P("gz", None),
        ),
        out_specs=(P(None, None, ("gx", "gy"), None, "gz"), P(None, ("gx", "gy"), None, "gz")),
        check_vma=False,
    )
```

```python
import jax
import jax.numpy as jnp
from jax import lax
from jax.experimental import pallas as pl
from jax.experimental.pallas import tpu as pltpu
from jax.sharding import PartitionSpec as P

COUPLING = 1.0 / 3.0
NEAR = 7.0 / 9.0
FAR = 1.0 / 36.0
F32 = jnp.float32
BF16 = jnp.bfloat16
MESH = pl.DeviceIdType.MESH
HIGH = lax.Precision.HIGHEST
CHUNKS = 4
OUT_CHUNKS = 6
PLANES = 8
MIB = 1 << 20


def split(values):
    high = values.astype(BF16)
    return high, (values - high.astype(F32)).astype(BF16)


def iota(shape, dim):
    return lax.broadcasted_iota(jnp.int32, shape, dim)


def band(size):
    step = iota((size, size), 1) - iota((size, size), 0)
    near = jnp.where(step == 1, NEAR, jnp.where(step == -1, -NEAR, 0.0))
    far = jnp.where(step == 2, FAR, jnp.where(step == -2, -FAR, 0.0))
    return (near + far).astype(F32)


def dot(a, b, dims=((1,), (0,)), precision=None):
    return lax.dot_general(a, b, (dims, ((), ())), precision=precision, preferred_element_type=F32)


def z_tables(z_inverse, metric, spread):
    size = z_inverse.shape[0]
    columns = z_inverse.T
    lines = [columns[k : k + 1] * metric for k in (0, 1, size - 2, size - 1)]
    row = iota((32, size), 0)
    zero = jnp.zeros((64, size), BF16)
    for field in range(6):
        table = jnp.zeros((32, size), F32)
        for k, line in enumerate(lines):
            table = jnp.where(row == 8 * k + field, line, table)
        high, low = split(table)
        spread[:, field * size : (field + 1) * size] = jnp.concatenate(
            [high, high, zero, low, low, zero], axis=0)


def z_weights(z_inverse, metric, weights):
    high, low = split(dot(z_inverse, band(z_inverse.shape[0]), precision=HIGH).T * metric)
    both = jnp.concatenate([high, low], axis=1)
    weights[...] = jnp.concatenate([both, both], axis=0)


def y_table(y_inverse, metric):
    size = y_inverse.shape[0]
    own = iota((size, size), 0) == iota((size, size), 1)
    column = jnp.sum(jnp.where(own, metric, 0.0), axis=1, keepdims=True)
    high, low = split(y_inverse)
    near, rest = split(band(size))
    product = dot(jnp.concatenate([high, low, high], axis=1), jnp.concatenate([near, near, rest], axis=0))
    high, low = split(product * column)
    return jnp.concatenate([high, high, low], axis=1)


def x_end_weights(inverse, store):
    size = inverse.shape[0]
    rows = size + 8
    step = iota((rows, size), 0) - iota((rows, size), 1) - 2
    near = jnp.where(step == 1, NEAR, jnp.where(step == -1, -NEAR, 0.0))
    far = jnp.where(step == 2, FAR, jnp.where(step == -2, -FAR, 0.0))
    taps = (near + far).astype(F32)
    for end, line in ((0, 0), (1, size - 1)):
        column = jnp.sum(taps * inverse[line : line + 1], axis=1, keepdims=True)
        store[end * rows : (end + 1) * rows] = jnp.broadcast_to(column, (rows, 128))


def x_tables(inverse, metric, corners, tab):
    size = inverse.shape[0]
    row, col = iota((size, size), 0), iota((size, size), 1)

    def pick(values, shift):
        return jnp.sum(jnp.where(col == row + shift, values, 0.0), axis=1, keepdims=True)

    def shifted(values, by):
        pad = jnp.zeros((1, values.shape[1]), F32)
        if by > 0:
            return jnp.concatenate([values[1:], pad], axis=0)
        return jnp.concatenate([pad, values[:-1]], axis=0)

    line = iota((size, 1), 0)
    below = shifted(inverse, 1)
    scale = pick(metric, 0)
    pivot = jnp.where(line < size - 1, pick(below, 1), 1.0)
    up = pick(inverse, 1) / pivot
    own = pick(inverse, 0) - up * pick(below, 0)
    before = jnp.where(line > 0, shifted(own, -1), 1.0)
    down = (pick(inverse, -1) - up * pick(below, -1)) / before
    above_scale = jnp.where(line < size - 1, pick(metric, 1), 1.0)
    below_scale = jnp.where(line > 0, pick(metric, -1), 1.0)
    for k, value in enumerate((NEAR * scale * own, down * scale / below_scale, up * scale / above_scale)):
        tab[k * size : (k + 1) * size] = jnp.broadcast_to(value, (size, 128))
    for side, end in ((0, 0), (1, size - 1)):
        own_end = inverse[end : end + 1, end : end + 1]
        other = corners[side]
        gain = (COUPLING / NEAR) / (1.0 - COUPLING * COUPLING * other * own_end)
        tab[3 * size + 16 * side : 3 * size + 16 * side + 8] = gain
        tab[3 * size + 16 * side + 8 : 3 * size + 16 * side + 16] = COUPLING * other * gain


def tile_of(table, row):
    return jnp.broadcast_to(table[row : row + 1], (8, 128))


def z_faces_of(v, corner, zs1):
    size, rows = v.shape[1:3]
    lane = iota((1, 128), 1)
    for k in range(2 * rows // 128):
        total = None
        for p in range(size // 2):
            for i in range(3):
                lines = v[i, 2 * p : 2 * p + 2].reshape(2 * rows, 128)[128 * k : 128 * k + 128]
                first = 16 * p + 4 * i
                moved = pltpu.roll(lines, first + 2, 1)
                total = moved if total is None else jnp.where((lane >= first) & (lane < first + 4), moved, total)
        got = total.T
        for p in range(size // 2):
            for side, layers in ((0, (2, 3)), (1, (0, 1))):
                lines = [got[16 * p + 4 * i + n : 16 * p + 4 * i + n + 1] for n in layers for i in range(3)]
                zs1[side, p, :, 128 * k : 128 * k + 128] = jnp.concatenate(
                    lines + [jnp.broadcast_to(corner[side], (1, 128)), jnp.zeros((1, 128), F32)], axis=0)


def z_ends_of(gather, inverse_metric, zs2):
    for k in range(gather.shape[0] // 128):
        got = gather[128 * k : 128 * k + 128].T
        for p in range(zs2.shape[1]):
            for side in range(2):
                lines = [got[16 * p + 2 * f + 1 - side : 16 * p + 2 * f + 2 - side] for f in range(6)]
                zs2[side, p, :, 128 * k : 128 * k + 128] = inverse_metric[side] * jnp.concatenate(
                    lines + [jnp.zeros((2, 128), F32)], axis=0)


def z_local(q, v, parts, ztab, gyz, cyz, gather):
    rows, cz = v.shape[2:]
    lane = iota((1, cz), 1)
    planes = [PLANES * q + k for k in range(PLANES)]
    for x in planes:
        velocity = [v[i, x] for i in range(3)]
        for field in range(6):
            value = velocity[field] if field < 3 else velocity[field - 3] * velocity[2]
            parts[field, x] = jnp.concatenate(split(value), axis=1)
    ends = [gather[k * rows : (k + 1) * rows] for k in range(2)]
    for k, x in enumerate(planes):
        got = dot(parts[:, x].reshape(6 * rows, 2 * cz), ztab[...])
        got = got[:, :cz] + got[:, cz:]
        for f in range(6):
            values = got[f * rows : (f + 1) * rows]
            if f < 3:
                gyz[1, f, x] = values
            else:
                cyz[f - 3, x] = values
            first = 8 * PLANES * q + 16 * (k // 2) + 2 * f
            kept = (lane >= first) & (lane < first + 2)
            ends[k % 2] = jnp.where(kept, pltpu.roll(values, first + 1, 1), ends[k % 2])
    for k in range(2):
        gather[k * rows : (k + 1) * rows] = ends[k]


def beside(halo, near, far):
    def six(first):
        lines = halo[first : first + 3]
        pad = jnp.zeros((2, lines.shape[1]), F32)
        return jnp.concatenate([lines, lines * lines[2:3], pad], axis=0)

    return six(near), six(far)


def z_halo(zh, z_inverse, zs2):
    size = z_inverse.shape[0]
    weights = []
    for line in (0, size - 1):
        a, b, c, d = (z_inverse[line : line + 1, k : k + 1] for k in (0, 1, size - 2, size - 1))
        weights.append((-NEAR * a - FAR * b, -FAR * a, NEAR * d + FAR * c, FAR * d))
    for p in range(zh.shape[1]):
        layers = beside(zh[0, p], 3, 0) + beside(zh[1, p], 0, 3)
        for side in range(2):
            total = zs2[side, p]
            for weight, layer in zip(weights[side], layers):
                total = total + weight * layer
            zs2[side, p] = total


def z_correct(q, spread, z_inverse, zh, zp, zs2, gyz, cyz):
    rows, cz = gyz.shape[3:]
    square = COUPLING * COUPLING
    own = (z_inverse[0:1, 0:1], z_inverse[cz - 1 : cz, cz - 1 : cz])
    lines = []
    for k in range(2):
        p = 2 * q + k
        terms = []
        for side, sign in ((0, -1.0), (1, 1.0)):
            halo = zh[side, p]
            near, far = beside(halo, 3 - 3 * side, 3 * side)
            other = halo[6:7, 0:1]
            gain = COUPLING / (1.0 - square * other * own[side])
            first = (sign * NEAR) * near + (sign * FAR) * far - gain * zp[side, p]
            first = first + (COUPLING * other * gain) * zs2[side, p]
            second = (sign * FAR) * near
            terms += [first, second] if side == 0 else [second, first]
        high, low = split(jnp.concatenate(terms, axis=0))
        lines += [high.astype(F32), low.astype(F32)]
    turned = jnp.concatenate(lines, axis=0).T
    turned = jnp.concatenate([turned, pltpu.roll(turned, 64, 1)], axis=0).astype(BF16)
    more = dot(jnp.concatenate([turned, turned], axis=1), spread[...])
    planes = pl.ds(4 * q, 4)
    for i in range(3):
        gyz[1, i, planes] = gyz[1, i, planes] + more[:, i * cz : (i + 1) * cz].reshape(4, rows, cz)
        cyz[i, planes] = cyz[i, planes] + more[:, (3 + i) * cz : (4 + i) * cz].reshape(4, rows, cz)


def x_local(t, v, wtab, xe):
    part = pl.ds(pl.multiple_of(t * 8, 8), 8)
    size = v.shape[1]
    ends = [[None] * 6, [None] * 6]
    for j in range(size):
        velocity = [v[i, j, part] for i in range(3)]
        fields = velocity + [a * velocity[0] for a in velocity]
        for end in range(2):
            weight = tile_of(wtab, end * (size + 8) + j + 2)
            for f in range(6):
                term = weight * fields[f]
                ends[end][f] = term if ends[end][f] is None else ends[end][f] + term
    for end in range(2):
        for f in range(6):
            xe[end, f, part] = ends[end][f]


def x_halo(t, size, xh, wtab, xe):
    part = pl.ds(pl.multiple_of(t * 8, 8), 8)
    ends = [[xe[end, f, part] for f in range(6)] for end in range(2)]
    for side in range(2):
        for layer in range(2):
            j = layer - 2 if side == 0 else size + layer
            velocity = [xh[side, i, layer, part] for i in range(3)]
            fields = velocity + [a * velocity[0] for a in velocity]
            for end in range(2):
                weight = tile_of(wtab, end * (size + 8) + j + 2)
                for f in range(6):
                    ends[end][f] = ends[end][f] + weight * fields[f]
    for end in range(2):
        for f in range(6):
            xe[end, f, part] = ends[end][f]


def along_y(q, v, parts, ytab, gyz, cyz):
    cz = v.shape[3]
    planes = [PLANES * q + k for k in range(PLANES)]

    def apply(pieces):
        high = jnp.concatenate([a[0] for a in pieces], axis=1)
        low = jnp.concatenate([a[1] for a in pieces], axis=1)
        return dot(ytab[...], jnp.concatenate([high, low, high], axis=0))

    def held(field):
        got = [parts[field, x] for x in planes]
        return [(g[:, :cz], g[:, cz:]) for g in got]

    for i in range(3):
        got = apply(held(i))
        for k, x in enumerate(planes):
            gyz[0, i, x] = got[:, k * cz : (k + 1) * cz]
        got = apply(held(4) if i == 2 else [split(v[i, x] * v[1, x]) for x in planes])
        for k, x in enumerate(planes):
            cyz[i, x] = cyz[i, x] + got[:, k * cz : (k + 1) * cz]


def times(body, start, stop, unit):
    @pl.loop(start // unit, stop // unit)
    def _(t):
        for k in range(unit):
            body(unit * t + k)


def exchange_kernel(
    v_hbm, xi_hbm, yi_hbm, zi_hbm, mx_hbm, my_hbm, mz_hbm,
    v, xh, xp, xe, tab, gyz, cyz,
    xi, yi, zi, mx, my, mz, xcs, xc, wtab, parts, zs1, zs2, zh, zp, gather, ytab, ztab, spread,
    load_sem, x1s, x1r, x2s, x2r, z1s, z1r, z2s, z2r, xcsem, xcrecv,
):
    gx, gy, gz = lax.axis_index("gx"), lax.axis_index("gy"), lax.axis_index("gz")
    nx, ny, nz = lax.axis_size("gx"), lax.axis_size("gy"), lax.axis_size("gz")
    me = gx * ny + gy
    count = nx * ny
    xl, xr = lax.rem(me + count - 1, count), lax.rem(me + 1, count)
    left = {"gx": xl // ny, "gy": lax.rem(xl, ny)}
    right = {"gx": xr // ny, "gy": lax.rem(xr, ny)}
    below = {"gz": lax.rem(gz + nz - 1, nz)}
    above = {"gz": lax.rem(gz + 1, nz)}
    barrier = pltpu.get_barrier_semaphore()
    for device in (left, right, below, above):
        pl.semaphore_signal(barrier, inc=1, device_id=device, device_id_type=MESH)

    loads = [
        pltpu.make_async_copy(src, dst, load_sem.at[k])
        for k, (src, dst) in enumerate(
            ((zi_hbm, zi), (xi_hbm, xi), (v_hbm, v), (yi_hbm, yi), (mx_hbm, mx), (my_hbm, my), (mz_hbm, mz)))
    ]
    for load in loads:
        load.start()
    cx, rows, cz = v.shape[1:]

    def send(src, dst, s, r, device):
        return pltpu.make_async_remote_copy(
            src_ref=src, dst_ref=dst, send_sem=s, recv_sem=r, device_id=device, device_id_type=MESH)

    step = rows // CHUNKS
    pl.semaphore_wait(barrier, 4)
    faces = []
    for c in range(CHUNKS):
        part = pl.ds(c * step, step)
        pair = (
            send(v_hbm.at[:, pl.ds(cx - 2, 2), part], xh.at[0, :, :, part], x1s.at[0, c], x1r.at[0, c], right),
            send(v_hbm.at[:, pl.ds(0, 2), part], xh.at[1, :, :, part], x1s.at[1, c], x1r.at[1, c], left),
        )
        for copy in pair:
            copy.start()
        faces.append(pair)
    loads[0].wait()
    loads[1].wait()
    loads[6].wait()
    z_inverse = zi[...]
    corner = (z_inverse[0:1, 0:1], z_inverse[cz - 1 : cz, cz - 1 : cz])
    z_weights(z_inverse, mz[...], ztab)
    x_inverse = xi[...]
    xcs[0] = jnp.broadcast_to(x_inverse[0:1, 0:1], (8, 128))
    xcs[1] = jnp.broadcast_to(x_inverse[cx - 1 : cx, cx - 1 : cx], (8, 128))
    x_end_weights(x_inverse, wtab)
    loads[2].wait()
    z_faces_of(v, corner, zs1)
    corners = (
        send(xcs.at[1], xc.at[0], xcsem.at[0], xcrecv.at[0], right),
        send(xcs.at[0], xc.at[1], xcsem.at[1], xcrecv.at[1], left),
    )
    for copy in corners:
        copy.start()
    z_faces = (
        send(zs1.at[1], zh.at[0], z1s.at[0], z1r.at[0], above),
        send(zs1.at[0], zh.at[1], z1s.at[1], z1r.at[1], below),
    )
    for copy in z_faces:
        copy.start()
    times(lambda t: x_local(t, v, wtab, xe), 0, rows // 8, 2)

    inverse_metric = (1.0 / mz[:, 0:1], 1.0 / mz[:, cz - 1 : cz])

    def z_pass(first, last):
        pl.loop(first, last)(lambda p: z_local(p, v, parts, ztab, gyz, cyz, gather))

    x_ends = []

    def x_pass(c):
        for copy in faces[c]:
            copy.wait()
        times(lambda t: x_halo(t, cx, xh, wtab, xe), c * (step // 8), (c + 1) * (step // 8), 2)
        part = pl.ds(c * step, step)
        pair = (
            send(xe.at[1, :, part], xp.at[0, :, part], x2s.at[0, c], x2r.at[0, c], right),
            send(xe.at[0, :, part], xp.at[1, :, part], x2s.at[1, c], x2r.at[1, c], left),
        )
        for copy in pair:
            copy.start()
        x_ends.append(pair)

    z_tables(z_inverse, mz[...], spread)
    gather[...] = jnp.zeros(gather.shape, F32)
    z_pass(0, cx // 2 // PLANES)
    x_pass(0)
    x_pass(1)
    z_pass(cx // 2 // PLANES, cx // PLANES)
    x_pass(2)
    for copy in z_faces:
        copy.wait()
    z_ends_of(gather, inverse_metric, zs2)
    z_halo(zh, z_inverse, zs2)
    z_ends = (
        send(zs2.at[1], zp.at[0], z2s.at[0], z2r.at[0], above),
        send(zs2.at[0], zp.at[1], z2s.at[1], z2r.at[1], below),
    )
    for copy in z_ends:
        copy.start()
    for c in range(3, CHUNKS):
        x_pass(c)
    for load in loads[3:6]:
        load.wait()
    ytab[...] = y_table(yi[...], my[...])

    def y_pass(first, last):
        pl.loop(first, last)(lambda q: along_y(q, v, parts, ytab, gyz, cyz))

    y_pass(0, cx // PLANES)
    for copy in z_ends:
        copy.wait()
    times(lambda q: z_correct(q, spread, z_inverse, zh, zp, zs2, gyz, cyz), 0, cx // 4, 2)
    for copy in corners:
        copy.wait()
    x_tables(x_inverse, mx[...], xc, tab)
    for pair in x_ends:
        for copy in pair:
            copy.wait()


def exchange(velocity, x_inverse, y_inverse, z_inverse, metric_x, metric_y, metric_z):
    _, cx, rows, cz = velocity.shape
    dma = pltpu.SemaphoreType.DMA

    def vmem(*shape):
        return pltpu.VMEM(shape, F32)

    def half(*shape):
        return pltpu.VMEM(shape, BF16)

    outs = (
        (3, cx, rows, cz),
        (2, 3, 2, rows, cz),
        (2, 6, rows, cz),
        (2, 6, rows, cz),
        (3 * cx + 32, 128),
        (2, 3, cx, rows, cz),
        (3, cx, rows, cz),
    )
    return pl.pallas_call(
        exchange_kernel,
        out_shape=tuple(jax.ShapeDtypeStruct(shape, F32) for shape in outs),
        in_specs=[pl.BlockSpec(memory_space=pltpu.HBM)] * 7,
        out_specs=(pl.BlockSpec(memory_space=pltpu.VMEM),) * len(outs),
        scratch_shapes=[
            vmem(cx, cx), vmem(rows, rows), vmem(cz, cz), vmem(1, cx), vmem(1, rows), vmem(1, cz),
            vmem(2, 8, 128), vmem(2, 8, 128), vmem(2 * (cx + 8), 128),
            half(6, cx, rows, 2 * cz),
            *[vmem(2, cx // 2, 8, 2 * rows)] * 4, vmem(2 * rows, cz),
            half(rows, 3 * rows), half(2 * cz, 2 * cz), half(256, 6 * cz),
            dma((7,)),
            dma((2, CHUNKS)), dma((2, CHUNKS)), dma((2, CHUNKS)), dma((2, CHUNKS)),
            dma((2,)), dma((2,)), dma((2,)), dma((2,)), dma((2,)), dma((2,)),
        ],
        compiler_params=pltpu.CompilerParams(
            collective_id=0, has_side_effects=True, vmem_limit_bytes=22 * MIB),
        name="exchange",
    )(*[
        pltpu.with_memory_space_constraint(a, pltpu.HBM)
        for a in (velocity, x_inverse, y_inverse, z_inverse, metric_x.reshape(1, cx),
                  metric_y.reshape(1, rows), metric_z.reshape(1, cz))
    ])


def x_sweep(part, v, xh, xp, xe, tab, gx, conv, cyz):
    cx = v.shape[1]

    def cell(j):
        if j < 0:
            velocity = [xh[0, i, j + 2, part] for i in range(3)]
        elif j >= cx:
            velocity = [xh[1, i, j - cx, part] for i in range(3)]
        else:
            velocity = [v[i, j, part] for i in range(3)]
        return velocity + [a * velocity[0] for a in velocity]

    window = [cell(j) for j in range(-2, 2)]
    state = None
    for j in range(cx):
        window.append(cell(j + 2))
        fresh = []
        for f in range(6):
            d = (window[3][f] - window[1][f]) + (FAR / NEAR) * (window[4][f] - window[0][f])
            for side, line in ((0, 0), (1, cx - 1)):
                if j == line:
                    k = 3 * cx + 16 * side
                    d = d - tab[k : k + 8] * xp[side, f, part] + tab[k + 8 : k + 16] * xe[side, f, part]
            value = tile_of(tab, j) * d
            if state is not None:
                value = value + tile_of(tab, cx + j) * state[f]
            fresh.append(value)
            if j < cx - 1:
                if f < 3:
                    gx[f, j, part] = value
                else:
                    conv[f - 3, j, part] = value
        state = fresh
        window.pop(0)
    for j in range(cx - 1, -1, -1):
        if j < cx - 1:
            up = tile_of(tab, 2 * cx + j)
            state = [(gx[f, j, part] if f < 3 else conv[f - 3, j, part]) + up * state[f] for f in range(6)]
        for i in range(3):
            gx[i, j, part] = state[i]
            conv[i, j, part] = state[3 + i] + cyz[i, j, part]


def x_kernel(v, xh, xp, xe, tab, gyz, cyz, grad, conv, gx_out, conv_out, yz_sem, x_sem, c_sem):
    rows = v.shape[2]
    copies = [pltpu.make_async_copy(gyz.at[k], grad.at[:, 1 + k], yz_sem.at[k]) for k in range(2)]
    for copy in copies:
        copy.start()
    step = rows // OUT_CHUNKS
    for c in range(OUT_CHUNKS):
        times(
            lambda t: x_sweep(
                pl.ds(pl.multiple_of(t * 8, 8), 8), v, xh, xp, xe, tab, gx_out, conv_out, cyz),
            c * (step // 8), (c + 1) * (step // 8), 2)
        part = pl.ds(c * step, step)
        pair = (
            pltpu.make_async_copy(gx_out.at[:, :, part], grad.at[:, 0, :, part], x_sem.at[c]),
            pltpu.make_async_copy(conv_out.at[:, :, part], conv.at[:, :, part], c_sem.at[c]),
        )
        for copy in pair:
            copy.start()
        copies += pair
    for copy in copies:
        copy.wait()


def x_solve(v, xh, xp, xe, tab, gyz, cyz):
    _, cx, rows, cz = v.shape
    dma = pltpu.SemaphoreType.DMA
    return pl.pallas_call(
        x_kernel,
        out_shape=(
            jax.ShapeDtypeStruct((3, 3, cx, rows, cz), F32),
            jax.ShapeDtypeStruct((3, cx, rows, cz), F32),
        ),
        in_specs=[pl.BlockSpec(memory_space=pltpu.VMEM)] * 7,
        out_specs=(pl.BlockSpec(memory_space=pltpu.HBM),) * 2,
        scratch_shapes=[
            pltpu.VMEM((3, cx, rows, cz), F32),
            pltpu.VMEM((3, cx, rows, cz), F32),
            dma((2,)), dma((OUT_CHUNKS,)), dma((OUT_CHUNKS,)),
        ],
        compiler_params=pltpu.CompilerParams(vmem_limit_bytes=14 * MIB),
        name="x_solve",
    )(v, xh, xp, xe, tab, gyz, cyz)


def on_device(velocity, metric_x, metric_y, metric_z, x_inverse, y_inverse, z_inverse):
    return tuple(x_solve(*exchange(
        velocity, x_inverse, y_inverse, z_inverse, metric_x, metric_y, metric_z)))


def solution(mesh):
    return jax.shard_map(
        on_device,
        mesh=mesh,
        in_specs=(
            P(None, ("gx", "gy"), None, "gz"),
            P(("gx", "gy")),
            P(),
            P("gz"),
            P(("gx", "gy"), None),
            P(),
            P("gz", None),
        ),
        out_specs=(P(None, None, ("gx", "gy"), None, "gz"), P(None, ("gx", "gy"), None, "gz")),
        check_vma=False,
    )
```
